32 devices in a mesh: ctx: 4 (over y, core), head: 2 (over x), dp: 4 (over z).
Axes of the slice: x: 2, y: 2, z: 4, core: 2. Of those that a mesh axis runs over, the one named last changes fastest.
Arguments:
- queries: bfloat16 [4096, 1024], P(('dp', 'ctx'), 'head'), parts along dimension 0, may hold values from -6 to 6
- keys: bfloat16 [4096, 1024], P(('dp', 'ctx'), 'head'), parts along dimension 0, may hold values from -6 to 6
- values: bfloat16 [4096, 1024], P(('dp', 'ctx'), 'head'), parts along dimension 0, may hold values from -6 to 6
- out_grad: bfloat16 [4096, 1024], P(('dp', 'ctx'), 'head'), parts along dimension 0, may hold values from -6 to 6
- random_blocks: int32 [32, 8, 3], P(('dp', 'head')), parts along dimension 0, may hold values from 0 to 7, as said below
- global_blocks: int32 [8], P('dp'), parts along dimension 0, may hold values from 0 to 7, as said below
Outputs:
- attended: bfloat16 [4096, 1024], P(('dp', 'ctx'), 'head'), parts along dimension 0
- query_grad: bfloat16 [4096, 1024], P(('dp', 'ctx'), 'head'), parts along dimension 0
- key_grad: bfloat16 [4096, 1024], P(('dp', 'ctx'), 'head'), parts along dimension 0
- value_grad: bfloat16 [4096, 1024], P(('dp', 'ctx'), 'head'), parts along dimension 0
The draws below stay inside these ranges and needn't reach their ends.
There are 4 independent parts, one for each index of `dp`. The reference program is written for one: setup_inputs(seed, part) draws one part's arguments, and reference() takes and returns one part's arrays. A program takes and returns all parts, laid end to end along the dimension named above; each array names one. Nothing has to cross between parts.
Inputs may be any that keep to these rules, and one draw needn't show every extreme that they name: `random_blocks`: cut the blocks into runs of 2 in order and the heads into runs of 4. For each run of heads and each run of query blocks, its 24 entries name blocks of any one run of blocks at most 6 times, and some run of blocks exactly 6 times. `global_blocks`: 2 different blocks.
All inputs are finite; a program needn't handle non-finite values.
Results may differ from the reference program's by a relative error of at most 0.015.
Values may be sent and summed in bfloat16 or wider, within the bound.
A program may use at most 64 MiB of HBM per device.

```python
import jax
import jax.numpy as jnp
from jax import lax

DH = 128
BS = 128
HEADS_DEV = 4
RAND = 3
GLOBAL = 2
BLK_DEV = 2
HEADS = 8
NB = 8
SEQ = 1024


def paired_tokens(key):
    base_key = jax.random.fold_in(key, 7)
    key_query, key_key = jax.random.split(base_key, 2)
    array_shape = (SEQ, HEADS * DH)
    query_out = jnp.clip(jax.random.normal(key_query, array_shape, jnp.float32), -6.0, 6.0)
    key_out = jnp.clip(jax.random.normal(key_key, array_shape, jnp.float32), -6.0, 6.0)
    return (query_out, key_out)


def draw_queries(key, part):
    return paired_tokens(key)[0].astype(jnp.bfloat16)


def draw_keys(key, part):
    return paired_tokens(key)[1].astype(jnp.bfloat16)


def draw_random_blocks(key, part):
    group_count = HEADS // HEADS_DEV
    device_count = NB // BLK_DEV
    entry_count = HEADS_DEV * BLK_DEV * RAND
    base_list = jnp.arange(entry_count, dtype=jnp.int32) % device_count
    split_keys = jax.random.split(jax.random.fold_in(key, 3), group_count * device_count)
    holders = jax.vmap(lambda single_key: jax.random.permutation(single_key, base_list))(split_keys)
    within = jax.random.randint(jax.random.fold_in(key, 5), (group_count * device_count, entry_count), 0, BLK_DEV)
    blocks = holders * BLK_DEV + within
    blocks = blocks.reshape(group_count, device_count, HEADS_DEV, BLK_DEV, RAND).transpose(0, 2, 1, 3, 4)
    return blocks.reshape(HEADS, NB, RAND).astype(jnp.int32)


def draw_global_blocks(key, part):
    return jax.random.permutation(jax.random.fold_in(key, 9), NB)[:GLOBAL].astype(jnp.int32)


def block_levels(stream_key, shape, shards, least, largest):
    factor_of = 1.0
    for position, shards_of in shards:
        draws = jax.random.uniform(jax.random.fold_in(jax.random.fold_in(stream_key, 6), position), (shards_of,), jnp.float32, least / len(shards), largest / len(shards))
        factor_of = factor_of * jnp.repeat(jnp.exp(draws), shape[position] // shards_of).reshape((-1,) + (1,) * (len(shape) - 1 - position))
    return factor_of


def centred(own_key, dims, spread, limit, shards=(), kind=jnp.bfloat16):
    array = jax.random.normal(own_key, dims, jnp.float32) * spread
    if len(shards) > 0:
        array = block_levels(own_key, dims, shards, -0.22, 0.18) * array
    return jnp.clip(array, min=-limit, max=limit).astype(kind)


def setup_inputs(seed: int = 0, part: int = 0) -> dict:
    key_of = jax.random.split(jax.random.key(seed), 7)
    own_keys = jax.random.split(jax.random.fold_in(key_of[6], part), 7)
    return {
        "queries": draw_queries(jax.random.fold_in(jax.random.fold_in(key_of[6], part), 71), part),
        "keys": draw_keys(jax.random.fold_in(jax.random.fold_in(key_of[6], part), 71), part),
        "values": centred(own_keys[2], (SEQ, HEADS * DH), 1.0, 6.0, ((0, 4), (1, 2))),
        "out_grad": centred(own_keys[3], (SEQ, HEADS * DH), 1.0, 6.0, ((0, 4), (1, 2))),
        "random_blocks": draw_random_blocks(jax.random.fold_in(jax.random.fold_in(key_of[6], part), 71), part),
        "global_blocks": draw_global_blocks(jax.random.fold_in(jax.random.fold_in(key_of[6], part), 71), part),
    }


def reference(queries, keys, values, out_grad, random_blocks, global_blocks):
    scaling = DH ** -0.5
    nblocks = SEQ // BS

    def to_heads(tensor):
        return tensor.reshape(nblocks, BS, HEADS, DH).transpose(2, 0, 1, 3)

    block_ids = jnp.arange(nblocks, dtype=jnp.int32)
    window = jnp.stack([(block_ids - 1) % nblocks, block_ids, (block_ids + 1) % nblocks], axis=1).astype(jnp.int32)
    glob_lists = jnp.broadcast_to(global_blocks[None, :], (nblocks, GLOBAL)).astype(jnp.int32)
    keep = 1.0 - jnp.sum((block_ids[:, None] == global_blocks[None, :]).astype(jnp.float32), axis=1)

    def one_head(inputs):
        head_q, head_k, head_v, head_g, head_random = inputs
        lists = jnp.concatenate([window, head_random.astype(jnp.int32), glob_lists], axis=1).astype(jnp.int32)
        nkeys = lists.shape[1]
        key_list = head_k[lists].reshape(nblocks, nkeys * BS, DH).astype(jnp.float32)
        value_list = head_v[lists].reshape(nblocks, nkeys * BS, DH).astype(jnp.float32)
        masked = head_g.astype(jnp.float32) * keep[:, None, None]
        scores = jnp.einsum("nqd,nkd->nqk", head_q.astype(jnp.float32), key_list) * scaling
        highest = jnp.max(scores, axis=-1, keepdims=True)
        logsum = highest + jnp.log(jnp.sum(jnp.exp(scores - highest), axis=-1, keepdims=True))
        probs = jnp.exp(scores - logsum).astype(jnp.bfloat16)
        output = jnp.einsum("nqk,nkd->nqd", probs.astype(jnp.float32), value_list).astype(jnp.bfloat16)
        deltas = jnp.sum(masked * output.astype(jnp.float32), axis=-1, keepdims=True)
        dprobs = jnp.einsum("nqd,nkd->nqk", masked, value_list)
        dscores = (probs.astype(jnp.float32) * (dprobs - deltas)).astype(jnp.bfloat16)
        dquery = jnp.einsum("nqk,nkd->nqd", dscores.astype(jnp.float32), key_list) * scaling
        dkl = jnp.einsum("nqk,nqd->nkd", dscores.astype(jnp.float32), head_q.astype(jnp.float32)) * scaling
        dvl = jnp.einsum("nqk,nqd->nkd", probs.astype(jnp.float32), masked)
        dkey = jnp.zeros((nblocks, BS, DH), jnp.float32).at[lists].add(dkl.reshape(nblocks, nkeys, BS, DH))
        dvalue = jnp.zeros((nblocks, BS, DH), jnp.float32).at[lists].add(dvl.reshape(nblocks, nkeys, BS, DH))
        glob_q = head_q[global_blocks].reshape(GLOBAL * BS, DH)
        glob_g = head_g[global_blocks].reshape(GLOBAL * BS, DH)
        flat_k = head_k.reshape(SEQ, DH)
        flat_v = head_v.reshape(SEQ, DH)
        gscores = jnp.dot(glob_q, flat_k.T, preferred_element_type=jnp.float32) * scaling
        ghigh = jnp.max(gscores, axis=-1, keepdims=True)
        glse = ghigh + jnp.log(jnp.sum(jnp.exp(gscores - ghigh), axis=-1, keepdims=True))
        gprobs = jnp.exp(gscores - glse).astype(jnp.bfloat16)
        gout = jnp.dot(gprobs, flat_v, preferred_element_type=jnp.float32).astype(jnp.bfloat16)
        gdelta = jnp.sum(glob_g.astype(jnp.float32) * gout.astype(jnp.float32), axis=-1, keepdims=True)
        gdprobs = jnp.dot(glob_g, flat_v.T, preferred_element_type=jnp.float32)
        gdscores = (gprobs.astype(jnp.float32) * (gdprobs - gdelta)).astype(jnp.bfloat16)
        gdquery = jnp.dot(gdscores, flat_k, preferred_element_type=jnp.float32) * scaling
        dkey = dkey + (jnp.dot(gdscores.T, glob_q, preferred_element_type=jnp.float32) * scaling).reshape(nblocks, BS, DH)
        dvalue = dvalue + jnp.dot(gprobs.T, glob_g, preferred_element_type=jnp.float32).reshape(nblocks, BS, DH)
        output = output.at[global_blocks].set(gout.reshape(GLOBAL, BS, DH))
        dquery = dquery.at[global_blocks].add(gdquery.reshape(GLOBAL, BS, DH))
        return output, dquery.astype(jnp.bfloat16), dkey.astype(jnp.bfloat16), dvalue.astype(jnp.bfloat16)

    results = lax.map(one_head, (to_heads(queries), to_heads(keys), to_heads(values), to_heads(out_grad), random_blocks))

    def to_rows(tensor):
        return tensor.transpose(1, 2, 0, 3).reshape(SEQ, HEADS * DH)

    return (to_rows(results[0]), to_rows(results[1]), to_rows(results[2]), to_rows(results[3]))
```

```python
import jax
import jax.numpy as jnp
from jax import lax
from jax.experimental import pallas as pl
from jax.experimental.pallas import tpu as pltpu
from jax.sharding import PartitionSpec as P

DH = 128
BS = 128
WIN = 3
RAND = 3
GLOBAL = 2


def broadcast(value, axis, source):
    kept = jnp.where(lax.axis_index(axis) == source, value, 0).astype(value.dtype)
    return lax.psum(kept, axis)


def merged(part, axis, combine):
    gathered = jax.tree.map(lambda a: lax.all_gather(a, axis), part)

    def take(source):
        return jax.tree.map(lambda a: lax.dynamic_index_in_dim(a, source, 0, False), gathered)

    return lax.fori_loop(
        1, lax.axis_size(axis), lambda source, state: combine(state, take(source)), take(0)
    )


def extended(value, sides, width):
    for axis, dim in sides:
        size, length = (lax.axis_size(axis), value.shape[dim])
        up = [(i, (i + 1) % size) for i in range(size)]
        down = [(j, i) for i, j in up]
        last = lax.slice_in_dim(value, length - width, length, axis=dim)
        first = lax.slice_in_dim(value, 0, width, axis=dim)
        before = lax.ppermute(last, axis, up)
        after = lax.ppermute(first, axis, down)
        value = jnp.concatenate([before, value, after], axis=dim)
    return value


def from_behind(value, axis, by):
    length = lax.axis_size(axis)
    return lax.ppermute(value, axis, [(i, (i + by) % length) for i in range(length)])


def picked(table, index):
    rows = lax.map(
        lambda one: lax.dynamic_index_in_dim(table, one, 0, False), index.reshape(-1)
    )
    return rows.reshape(index.shape + table.shape[1:])


def combine_stats(first_pair, second_pair):
    highest = jnp.maximum(first_pair[0], second_pair[0])
    summed = first_pair[1] * jnp.exp(first_pair[0] - highest) + second_pair[1] * jnp.exp(
        second_pair[0] - highest
    )
    return (highest, summed)


def sparse_rows(query_head, key_list, value_list, grad_head, scaling):
    scores = (
        jnp.einsum("nqd,nkd->nqk", query_head, key_list, preferred_element_type=jnp.float32)
        * scaling
    )
    highest = jnp.max(scores, axis=-1, keepdims=True)
    logsum = highest + jnp.log(jnp.sum(jnp.exp(scores - highest), axis=-1, keepdims=True))
    probs = jnp.exp(scores - logsum).astype(jnp.bfloat16)
    output = jnp.einsum(
        "nqk,nkd->nqd", probs, value_list, preferred_element_type=jnp.float32
    ).astype(jnp.bfloat16)
    deltas = jnp.sum(
        grad_head.astype(jnp.float32) * output.astype(jnp.float32), axis=-1, keepdims=True
    )
    dprobs = jnp.einsum("nqd,nkd->nqk", grad_head, value_list, preferred_element_type=jnp.float32)
    dscores = (probs.astype(jnp.float32) * (dprobs - deltas)).astype(jnp.bfloat16)
    dquery = (
        jnp.einsum("nqk,nkd->nqd", dscores, key_list, preferred_element_type=jnp.float32) * scaling
    )
    return (output, logsum[..., 0], deltas[..., 0], probs, dscores, dquery)


def on_device(queries, keys, values, out_grad, random_blocks, global_blocks):
    ctx_count = lax.axis_size("ctx")
    own_index = lax.axis_index("ctx")
    head_count = random_blocks.shape[0]
    local_rows = queries.shape[0]
    block_count = local_rows // BS
    features = queries.shape[1]
    scaling = DH ** (-0.5)
    entry_count = head_count * block_count * RAND
    capacity = (entry_count + ctx_count - 1) // ctx_count
    block_ids = own_index * block_count + jnp.arange(block_count, dtype=jnp.int32)
    global_hit = (block_ids[:, None] == global_blocks[None, :]).astype(jnp.float32)
    keep_rows = 1.0 - jnp.sum(global_hit, axis=1)
    stacked = jnp.stack([queries, keys, values, out_grad], axis=0)
    received = []
    for position in range(GLOBAL):
        holder_index = global_blocks[position] // block_count
        offset = global_blocks[position] % block_count * BS
        block_piece = lax.dynamic_slice_in_dim(stacked, offset, BS, axis=1)
        received.append(broadcast(block_piece, "ctx", holder_index))
    global_data = jnp.stack(received, axis=1).reshape(4, GLOBAL * BS, head_count, DH)
    global_query = global_data[0]
    global_key = global_data[1]
    global_value = global_data[2]
    global_grad = global_data[3]
    keys_split = keys.reshape(local_rows, head_count, DH)
    values_split = values.reshape(local_rows, head_count, DH)
    global_scores = (
        jnp.einsum("qhd,khd->hqk", global_query, keys_split, preferred_element_type=jnp.float32)
        * scaling
    )
    local_max = jnp.max(global_scores, axis=-1)
    local_sum = jnp.sum(jnp.exp(global_scores - local_max[..., None]), axis=-1)
    merged_max, merged_sum = merged((local_max, local_sum), "ctx", combine_stats)
    global_lse = merged_max + jnp.log(merged_sum)
    global_probs = jnp.exp(global_scores - global_lse[..., None]).astype(jnp.bfloat16)
    partial_out = jnp.einsum(
        "hqk,khd->qhd", global_probs, values_split, preferred_element_type=jnp.float32
    )
    global_out = lax.psum(partial_out, "ctx").astype(jnp.bfloat16)
    global_delta = jnp.sum(
        global_grad.astype(jnp.float32) * global_out.astype(jnp.float32), axis=-1
    ).T
    global_dprobs = jnp.einsum(
        "qhd,khd->hqk", global_grad, values_split, preferred_element_type=jnp.float32
    )
    global_dscores = (
        global_probs.astype(jnp.float32) * (global_dprobs - global_delta[..., None])
    ).astype(jnp.bfloat16)
    query_part = (
        jnp.einsum("hqk,khd->qhd", global_dscores, keys_split, preferred_element_type=jnp.float32)
        * scaling
    )
    key_from_global = (
        jnp.einsum("hqk,qhd->khd", global_dscores, global_query, preferred_element_type=jnp.float32)
        * scaling
    )
    value_from_global = jnp.einsum(
        "hqk,qhd->khd", global_probs, global_grad, preferred_element_type=jnp.float32
    )
    paired = jnp.stack([keys, values], axis=1)
    padded = extended(paired, (("ctx", 0),), BS)
    padded = padded.reshape(block_count + 2, BS, 2, head_count, DH)
    window = jnp.concatenate(
        [padded[start_block : start_block + block_count] for start_block in range(WIN)], axis=1
    )
    window = window.transpose(2, 3, 0, 1, 4)
    entry_blocks = (
        random_blocks.reshape(head_count, ctx_count, block_count, RAND)
        .transpose(1, 0, 2, 3)
        .reshape(ctx_count, entry_count)
    )
    owner_of = entry_blocks // block_count
    local_of = entry_blocks % block_count
    entry_ids = jnp.arange(entry_count, dtype=jnp.int32)
    head_of = entry_ids // (block_count * RAND)
    onehot = (owner_of[:, :, None] == jnp.arange(ctx_count, dtype=jnp.int32)[None, None, :]).astype(
        jnp.int32
    )
    before = jnp.cumsum(onehot, axis=1) - onehot
    rank_of = jnp.sum(before * onehot, axis=2)
    slot_hit = (owner_of == own_index)[:, :, None] & (
        rank_of[:, :, None] == jnp.arange(capacity, dtype=jnp.int32)[None, None, :]
    )
    send_index = jnp.sum(
        jnp.where(slot_hit, (local_of * head_count + head_of[None, :])[:, :, None], 0), axis=1
    )
    my_owner = lax.dynamic_index_in_dim(owner_of, own_index, axis=0, keepdims=False)
    my_rank = lax.dynamic_index_in_dim(rank_of, own_index, axis=0, keepdims=False)
    my_place = my_owner * capacity + my_rank
    masked_grad = (
        out_grad.reshape(block_count, BS, features) * keep_rows.astype(jnp.bfloat16)[:, None, None]
    ).reshape(local_rows, features)

    def to_table(tensor):
        return (
            tensor.reshape(block_count, BS, head_count, DH)
            .transpose(0, 2, 1, 3)
            .reshape(block_count * head_count, BS, DH)
        )

    send_keys = picked(to_table(keys), send_index)
    send_values = picked(to_table(values), send_index)
    got_keys, got_values = (
        lax.all_to_all(send_keys, "ctx", split_axis=0, concat_axis=0, tiled=True),
        lax.all_to_all(send_values, "ctx", split_axis=0, concat_axis=0, tiled=True),
    )
    random_keys = picked(got_keys.reshape(ctx_count * capacity, BS, DH), my_place).reshape(
        head_count, block_count, RAND * BS, DH
    )
    random_values = picked(got_values.reshape(ctx_count * capacity, BS, DH), my_place).reshape(
        head_count, block_count, RAND * BS, DH
    )
    query_heads = queries.reshape(block_count, BS, head_count, DH).transpose(2, 0, 1, 3)
    grad_heads = masked_grad.reshape(block_count, BS, head_count, DH).transpose(2, 0, 1, 3)
    global_key_heads = global_key.transpose(1, 0, 2)
    global_value_heads = global_value.transpose(1, 0, 2)
    window_cols = WIN * BS
    random_end = (WIN + RAND) * BS

    def head_work(inputs):
        (
            query_head,
            grad_head,
            win_keys,
            win_values,
            rand_keys,
            rand_values,
            glob_keys,
            glob_values,
        ) = inputs
        key_list = jnp.concatenate(
            [
                win_keys,
                rand_keys,
                jnp.broadcast_to(glob_keys[None], (block_count,) + glob_keys.shape),
            ],
            axis=1,
        )
        value_list = jnp.concatenate(
            [
                win_values,
                rand_values,
                jnp.broadcast_to(glob_values[None], (block_count,) + glob_values.shape),
            ],
            axis=1,
        )
        output, logsum, deltas, probs, dscores, dquery = sparse_rows(
            query_head, key_list, value_list, grad_head, scaling
        )
        win_dk = (
            jnp.einsum(
                "nqk,nqd->nkd",
                dscores[:, :, :window_cols],
                query_head,
                preferred_element_type=jnp.float32,
            )
            * scaling
        )
        win_dv = jnp.einsum(
            "nqk,nqd->nkd", probs[:, :, :window_cols], grad_head, preferred_element_type=jnp.float32
        )
        glob_dk = (
            jnp.einsum(
                "nqk,nqd->kd",
                dscores[:, :, random_end:],
                query_head,
                preferred_element_type=jnp.float32,
            )
            * scaling
        )
        glob_dv = jnp.einsum(
            "nqk,nqd->kd", probs[:, :, random_end:], grad_head, preferred_element_type=jnp.float32
        )
        win_dk = win_dk.reshape(block_count, WIN, BS, DH)
        win_dv = win_dv.reshape(block_count, WIN, BS, DH)
        ext_dk = sum(
            (
                jnp.pad(win_dk[:, shift_by], ((shift_by, WIN - 1 - shift_by), (0, 0), (0, 0)))
                for shift_by in range(WIN)
            )
        )
        ext_dv = sum(
            (
                jnp.pad(win_dv[:, shift_by], ((shift_by, WIN - 1 - shift_by), (0, 0), (0, 0)))
                for shift_by in range(WIN)
            )
        )
        rand_dk = (
            jnp.einsum(
                "nqk,nqd->nkd",
                dscores[:, :, window_cols:random_end],
                query_head,
                preferred_element_type=jnp.float32,
            )
            * scaling
        )
        rand_dv = jnp.einsum(
            "nqk,nqd->nkd",
            probs[:, :, window_cols:random_end],
            grad_head,
            preferred_element_type=jnp.float32,
        )
        return (output, logsum, deltas, dquery, ext_dk, ext_dv, glob_dk, glob_dv, rand_dk, rand_dv)

    results = lax.map(
        head_work,
        (
            query_heads,
            grad_heads,
            window[0],
            window[1],
            random_keys,
            random_values,
            global_key_heads,
            global_value_heads,
        ),
    )
    output_heads, logsums, deltas, dquery_heads, ext_dk, ext_dv, glob_dk, glob_dv = results[:8]
    query_total, glob_dk_total, glob_dv_total = lax.psum((query_part, glob_dk, glob_dv), "ctx")
    rim_low = jnp.stack([ext_dk[:, 0], ext_dv[:, 0]], axis=0)
    rim_high = jnp.stack([ext_dk[:, block_count + 1], ext_dv[:, block_count + 1]], axis=0)
    from_next = from_behind(rim_low.astype(jnp.bfloat16), "ctx", -1).astype(rim_low.dtype)
    from_prev = from_behind(rim_high.astype(jnp.bfloat16), "ctx", 1).astype(rim_high.dtype)
    key_heads = ext_dk[:, 1 : block_count + 1]
    value_heads = ext_dv[:, 1 : block_count + 1]
    key_heads = key_heads.at[:, 0].add(from_prev[0]).at[:, block_count - 1].add(from_next[0])
    value_heads = value_heads.at[:, 0].add(from_prev[1]).at[:, block_count - 1].add(from_next[1])
    rand_dk = results[8].reshape(entry_count, BS, DH)
    rand_dv = results[9].reshape(entry_count, BS, DH)
    out_keys = (
        jnp.zeros((ctx_count * capacity, BS, DH), jnp.float32)
        .at[my_place]
        .set(rand_dk)
        .reshape(ctx_count, capacity, BS, DH)
    )
    out_values = (
        jnp.zeros((ctx_count * capacity, BS, DH), jnp.float32)
        .at[my_place]
        .set(rand_dv)
        .reshape(ctx_count, capacity, BS, DH)
    )
    back_keys, back_values = (
        lax.all_to_all(out_keys, "ctx", split_axis=0, concat_axis=0, tiled=True),
        lax.all_to_all(out_values, "ctx", split_axis=0, concat_axis=0, tiled=True),
    )
    back_keys = back_keys.reshape(ctx_count * capacity, BS, DH)
    back_values = back_values.reshape(ctx_count * capacity, BS, DH)
    flat_index = send_index.reshape(-1)
    table_keys = (
        jnp.zeros((block_count * head_count, BS, DH), jnp.float32).at[flat_index].add(back_keys)
    )
    table_values = (
        jnp.zeros((block_count * head_count, BS, DH), jnp.float32).at[flat_index].add(back_values)
    )
    key_heads = key_heads + table_keys.reshape(block_count, head_count, BS, DH).transpose(
        1, 0, 2, 3
    )
    value_heads = value_heads + table_values.reshape(block_count, head_count, BS, DH).transpose(
        1, 0, 2, 3
    )

    def place_global(tensor):
        return jnp.sum(global_hit[None, :, :, None, None] * tensor[:, None], axis=2)

    key_heads = key_heads + place_global(glob_dk_total.reshape(head_count, GLOBAL, BS, DH))
    value_heads = value_heads + place_global(glob_dv_total.reshape(head_count, GLOBAL, BS, DH))
    key_heads = key_heads + key_from_global.reshape(block_count, BS, head_count, DH).transpose(
        2, 0, 1, 3
    )
    value_heads = value_heads + value_from_global.reshape(
        block_count, BS, head_count, DH
    ).transpose(2, 0, 1, 3)
    query_heads_total = dquery_heads + place_global(
        query_total.reshape(GLOBAL, BS, head_count, DH).transpose(2, 0, 1, 3)
    )
    output_total = output_heads.astype(jnp.float32) * keep_rows[None, :, None, None]
    output_total = output_total + place_global(
        global_out.astype(jnp.float32).reshape(GLOBAL, BS, head_count, DH).transpose(2, 0, 1, 3)
    )

    def to_rows(tensor):
        return tensor.transpose(1, 2, 0, 3).reshape(local_rows, features).astype(jnp.bfloat16)

    return (
        to_rows(output_total),
        to_rows(query_heads_total),
        to_rows(key_heads),
        to_rows(value_heads),
    )


Q, K, V, G = range(4)
LOG2E = 1.4426950408889634
VMEM_LIMIT = 40 * 1024 * 1024
GROUP = 4


def peer(step):
    me = lax.axis_index("ctx")
    return (me // 2 + step // 2) % 2 * 2 + (me % 2 + step % 2) % 2


def heads_kernel(
    random_ref,
    global_ref,
    q_ref,
    k_ref,
    v_ref,
    g_ref,
    att_ref,
    dq_ref,
    dk_ref,
    dv_ref,
    inb,
    outb,
    probs_buf,
    att_buf,
    dk_acc,
    dv_acc,
    bias,
    k_t,
    v_t,
    own_in,
    own_out,
    in_send,
    in_recv,
    out_send,
    out_recv,
    relay,
):
    n = GROUP
    me = lax.axis_index("ctx")
    rows = q_ref.shape[0]
    seq = n * rows
    blocks = seq // BS
    scaling = DH ** (-0.5)
    sources = (q_ref, k_ref, v_ref, g_ref)
    targets = (att_ref, dq_ref, dk_ref, dv_ref)

    def at_rows(device):
        return pl.ds(pl.multiple_of(device * rows, rows), rows)

    def at_head(device):
        return pl.ds(pl.multiple_of(device * DH, DH), DH)

    def in_copy(array, step, land):
        other = peer(step)
        return pltpu.make_async_remote_copy(
            src_ref=sources[array].at[:, at_head(other)],
            dst_ref=inb.at[array, at_rows(land)],
            send_sem=in_send.at[array, step - 1],
            recv_sem=in_recv.at[array, step - 1],
            device_id={"ctx": other},
            device_id_type=pl.DeviceIdType.MESH,
        )

    def out_copy(array, step, land):
        other = peer(step)
        return pltpu.make_async_remote_copy(
            src_ref=outb.at[array, at_rows(other)],
            dst_ref=targets[array].at[:, at_head(land)],
            send_sem=out_send.at[array, step - 1],
            recv_sem=out_recv.at[array, step - 1],
            device_id={"ctx": other},
            device_id_type=pl.DeviceIdType.MESH,
        )

    def own_copy_in(array):
        return pltpu.make_async_copy(
            sources[array].at[:, at_head(me)], inb.at[array, at_rows(me)], own_in.at[array]
        )

    def own_copy_out(array):
        return pltpu.make_async_copy(
            outb.at[array, at_rows(me)], targets[array].at[:, at_head(me)], own_out.at[array]
        )

    def arrived(array, step):
        if step == 0:
            own_copy_in(array).wait()
        else:
            in_copy(array, step, peer(step)).wait_recv()

    def leave(array, step):
        (own_copy_out(array) if step == 0 else out_copy(array, step, me)).start()

    barrier = pltpu.get_barrier_semaphore()
    for step in (2, 3):
        pl.semaphore_signal(
            barrier,
            inc=1,
            device_id={"ctx": peer(step)},
            device_id_type=pl.DeviceIdType.MESH,
        )
    for array in (K, V, Q, G):
        own_copy_in(array).start()
    pl.semaphore_wait(barrier, 2)
    for array in (K, V, Q, G):
        for step in (2, 3):
            in_copy(array, step, me).start()
    pl.semaphore_signal(
        relay, inc=1, device_id={"ctx": peer(2)}, device_id_type=pl.DeviceIdType.MESH
    )
    pl.semaphore_wait(relay, 1)
    for array in (K, V, Q, G):
        in_copy(array, 1, me).start()

    key_block = lax.broadcasted_iota(jnp.int32, (blocks, BS), 0)
    first, second = (global_ref[0], global_ref[1])
    per_device = rows // BS
    for block in range(blocks):
        query_block = jnp.full((blocks, BS), block, jnp.int32)
        named = [(block - 1) % blocks, block, (block + 1) % blocks]
        named += [random_ref[entry, me, block] for entry in range(RAND)]
        named += [first, second]
        count = sum((key_block == one).astype(jnp.int32) for one in named)
        is_global = (query_block == first) | (query_block == second)
        count = jnp.where(is_global, 1, count).astype(jnp.float32)
        level = jnp.where(count > 0.5, jnp.log2(jnp.maximum(count, 1.0)), -1e30)
        lanes = slice(block % per_device * BS, block % per_device * BS + BS)
        bias[block // per_device, :, lanes] = level

    contract_last = (((1,), (1,)), ((), ()))

    def weigh(step):
        arrived(Q, step)
        owner = peer(step)
        query = inb[Q, at_rows(owner)]
        scores = lax.dot_general(inb[K], query, contract_last, preferred_element_type=jnp.float32)
        scores = scores.reshape(blocks, BS, rows) * (scaling * LOG2E) + bias[owner][:, None, :]
        highest = jnp.max(scores, axis=(0, 1), keepdims=True)
        weights = jnp.exp2(scores - highest)
        total = jnp.sum(weights, axis=(0, 1), keepdims=True)
        probs = (weights * (1.0 / total)).reshape(seq, rows).astype(jnp.bfloat16)
        probs_buf[step] = probs

    def attend(step):
        att_t = jnp.dot(v_t[...], probs_buf[step], preferred_element_type=jnp.float32)
        att_t = att_t.astype(jnp.bfloat16).astype(jnp.float32)
        outb[0, at_rows(peer(step))] = att_t.T.astype(jnp.bfloat16)
        att_buf[step] = att_t
        leave(0, step)

    def differentiate(step):
        arrived(G, step)
        owner = peer(step)
        query = inb[Q, at_rows(owner)]
        grad = inb[G, at_rows(owner)]
        probs = probs_buf[step]
        delta = jnp.sum(grad.astype(jnp.float32).T * att_buf[step], axis=0, keepdims=True)
        dprobs = lax.dot_general(inb[V], grad, contract_last, preferred_element_type=jnp.float32)
        dscores = (probs.astype(jnp.float32) * (dprobs - delta)).astype(jnp.bfloat16)
        dq_t = jnp.dot(k_t[...], dscores, preferred_element_type=jnp.float32) * scaling
        outb[1, at_rows(owner)] = dq_t.T.astype(jnp.bfloat16)
        leave(1, step)
        dv = jnp.dot(probs, grad, preferred_element_type=jnp.float32)
        dk = jnp.dot(dscores, query, preferred_element_type=jnp.float32)
        dv_acc[...] = dv if step == 0 else dv_acc[...] + dv
        dk_acc[...] = dk if step == 0 else dk_acc[...] + dk

    for step in range(n):
        arrived(K, step)
    k_t[...] = inb[K].T
    weigh(0)
    weigh(1)
    for step in range(n):
        arrived(V, step)
    v_t[...] = inb[V].T
    for step in (0, 1):
        attend(step)
        differentiate(step)
    for step in (2, 3):
        weigh(step)
        attend(step)
    for step in (2, 3):
        differentiate(step)

    outb[2] = (dk_acc[...] * scaling).astype(jnp.bfloat16)
    outb[3] = dv_acc[...].astype(jnp.bfloat16)
    for step in (2, 3, 1, 0):
        for array in (2, 3):
            leave(array, step)

    for array in range(4):
        own_copy_out(array).wait()
        for step in range(1, n):
            in_copy(array, step, me).wait_send()
            out_copy(array, step, me).wait_send()
            out_copy(array, step, peer(step)).wait_recv()


def place_kernel(*refs):
    copies = [
        pltpu.make_async_copy(refs[array], refs[4 + array], refs[8].at[array])
        for array in range(4)
    ]
    for copy in copies:
        copy.start()
    for copy in copies:
        copy.wait()


def by_heads(queries, keys, values, out_grad, random_blocks, global_blocks):
    n = GROUP
    rows, features = queries.shape
    seq = n * rows
    blocks = seq // BS
    anywhere = pl.BlockSpec(memory_space=pl.ANY)
    scalars = pl.BlockSpec(memory_space=pltpu.SMEM)
    results = pl.pallas_call(
        heads_kernel,
        out_shape=[jax.ShapeDtypeStruct((rows, features), jnp.bfloat16)] * 4,
        in_specs=[scalars] * 2 + [anywhere] * 4,
        out_specs=[anywhere] * 4,
        scratch_shapes=[
            pltpu.VMEM((4, seq, DH), jnp.bfloat16),
            pltpu.VMEM((4, seq, DH), jnp.bfloat16),
            pltpu.VMEM((n, seq, rows), jnp.bfloat16),
            pltpu.VMEM((n, DH, rows), jnp.float32),
            pltpu.VMEM((seq, DH), jnp.float32),
            pltpu.VMEM((seq, DH), jnp.float32),
            pltpu.VMEM((n, blocks, rows), jnp.float32),
            pltpu.VMEM((DH, seq), jnp.bfloat16),
            pltpu.VMEM((DH, seq), jnp.bfloat16),
            pltpu.SemaphoreType.DMA((4,)),
            pltpu.SemaphoreType.DMA((4,)),
            pltpu.SemaphoreType.DMA((4, n - 1)),
            pltpu.SemaphoreType.DMA((4, n - 1)),
            pltpu.SemaphoreType.DMA((4, n - 1)),
            pltpu.SemaphoreType.DMA((4, n - 1)),
            pltpu.SemaphoreType.REGULAR,
        ],
        compiler_params=pltpu.CompilerParams(
            collective_id=0, has_side_effects=True, vmem_limit_bytes=VMEM_LIMIT
        ),
    )(
        *(
            pltpu.with_memory_space_constraint(array, pltpu.HBM)
            for array in (
                random_blocks.transpose(2, 0, 1),
                global_blocks,
                queries,
                keys,
                values,
                out_grad,
            )
        )
    )
    return pl.pallas_call(
        place_kernel,
        out_shape=[jax.ShapeDtypeStruct((rows, features), jnp.bfloat16)] * 4,
        in_specs=[anywhere] * 4,
        out_specs=[anywhere] * 4,
        scratch_shapes=[pltpu.SemaphoreType.DMA((4,))],
        compiler_params=pltpu.CompilerParams(vmem_limit_bytes=VMEM_LIMIT),
    )(*results)


def solution(mesh):
    in_specs = (
        P(("dp", "ctx"), "head"),
        P(("dp", "ctx"), "head"),
        P(("dp", "ctx"), "head"),
        P(("dp", "ctx"), "head"),
        P(("dp", "head"), None, None),
        P("dp"),
    )
    out_specs = (
        P(("dp", "ctx"), "head"),
        P(("dp", "ctx"), "head"),
        P(("dp", "ctx"), "head"),
        P(("dp", "ctx"), "head"),
    )
    ctx_count = mesh.shape["ctx"]

    def body(queries, *rest):
        heads = queries.shape[1] // DH
        if heads == ctx_count == GROUP:
            return by_heads(queries, *rest)
        return on_device(queries, *rest)

    return jax.shard_map(
        body, mesh=mesh, in_specs=in_specs, out_specs=out_specs, check_vma=False
    )
```

```python
import jax
import jax.numpy as jnp
from jax import lax
from jax.experimental import pallas as pl
from jax.experimental.pallas import tpu as pltpu
from jax.sharding import PartitionSpec as P

DH = 128
BS = 128
WIN = 3
RAND = 3
GLOBAL = 2


def broadcast(value, axis, source):
    kept = jnp.where(lax.axis_index(axis) == source, value, 0).astype(value.dtype)
    return lax.psum(kept, axis)


def merged(part, axis, combine):
    gathered = jax.tree.map(lambda a: lax.all_gather(a, axis), part)

    def take(source):
        return jax.tree.map(lambda a: lax.dynamic_index_in_dim(a, source, 0, False), gathered)

    return lax.fori_loop(
        1, lax.axis_size(axis), lambda source, state: combine(state, take(source)), take(0)
    )


def extended(value, sides, width):
    for axis, dim in sides:
        size, length = (lax.axis_size(axis), value.shape[dim])
        up = [(i, (i + 1) % size) for i in range(size)]
        down = [(j, i) for i, j in up]
        last = lax.slice_in_dim(value, length - width, length, axis=dim)
        first = lax.slice_in_dim(value, 0, width, axis=dim)
        before = lax.ppermute(last, axis, up)
        after = lax.ppermute(first, axis, down)
        value = jnp.concatenate([before, value, after], axis=dim)
    return value


def from_behind(value, axis, by):
    length = lax.axis_size(axis)
    return lax.ppermute(value, axis, [(i, (i + by) % length) for i in range(length)])


def picked(table, index):
    rows = lax.map(
        lambda one: lax.dynamic_index_in_dim(table, one, 0, False), index.reshape(-1)
    )
    return rows.reshape(index.shape + table.shape[1:])


def combine_stats(first_pair, second_pair):
    highest = jnp.maximum(first_pair[0], second_pair[0])
    summed = first_pair[1] * jnp.exp(first_pair[0] - highest) + second_pair[1] * jnp.exp(
        second_pair[0] - highest
    )
    return (highest, summed)


def sparse_rows(query_head, key_list, value_list, grad_head, scaling):
    scores = (
        jnp.einsum("nqd,nkd->nqk", query_head, key_list, preferred_element_type=jnp.float32)
        * scaling
    )
    highest = jnp.max(scores, axis=-1, keepdims=True)
    logsum = highest + jnp.log(jnp.sum(jnp.exp(scores - highest), axis=-1, keepdims=True))
    probs = jnp.exp(scores - logsum).astype(jnp.bfloat16)
    output = jnp.einsum(
        "nqk,nkd->nqd", probs, value_list, preferred_element_type=jnp.float32
    ).astype(jnp.bfloat16)
    deltas = jnp.sum(
        grad_head.astype(jnp.float32) * output.astype(jnp.float32), axis=-1, keepdims=True
    )
    dprobs = jnp.einsum("nqd,nkd->nqk", grad_head, value_list, preferred_element_type=jnp.float32)
    dscores = (probs.astype(jnp.float32) * (dprobs - deltas)).astype(jnp.bfloat16)
    dquery = (
        jnp.einsum("nqk,nkd->nqd", dscores, key_list, preferred_element_type=jnp.float32) * scaling
    )
    return (output, logsum[..., 0], deltas[..., 0], probs, dscores, dquery)


def on_device(queries, keys, values, out_grad, random_blocks, global_blocks):
    ctx_count = lax.axis_size("ctx")
    own_index = lax.axis_index("ctx")
    head_count = random_blocks.shape[0]
    local_rows = queries.shape[0]
    block_count = local_rows // BS
    features = queries.shape[1]
    scaling = DH ** (-0.5)
    entry_count = head_count * block_count * RAND
    capacity = (entry_count + ctx_count - 1) // ctx_count
    block_ids = own_index * block_count + jnp.arange(block_count, dtype=jnp.int32)
    global_hit = (block_ids[:, None] == global_blocks[None, :]).astype(jnp.float32)
    keep_rows = 1.0 - jnp.sum(global_hit, axis=1)
    stacked = jnp.stack([queries, keys, values, out_grad], axis=0)
    received = []
    for position in range(GLOBAL):
        holder_index = global_blocks[position] // block_count
        offset = global_blocks[position] % block_count * BS
        block_piece = lax.dynamic_slice_in_dim(stacked, offset, BS, axis=1)
        received.append(broadcast(block_piece, "ctx", holder_index))
    global_data = jnp.stack(received, axis=1).reshape(4, GLOBAL * BS, head_count, DH)
    global_query = global_data[0]
    global_key = global_data[1]
    global_value = global_data[2]
    global_grad = global_data[3]
    keys_split = keys.reshape(local_rows, head_count, DH)
    values_split = values.reshape(local_rows, head_count, DH)
    global_scores = (
        jnp.einsum("qhd,khd->hqk", global_query, keys_split, preferred_element_type=jnp.float32)
        * scaling
    )
    local_max = jnp.max(global_scores, axis=-1)
    local_sum = jnp.sum(jnp.exp(global_scores - local_max[..., None]), axis=-1)
    merged_max, merged_sum = merged((local_max, local_sum), "ctx", combine_stats)
    global_lse = merged_max + jnp.log(merged_sum)
    global_probs = jnp.exp(global_scores - global_lse[..., None]).astype(jnp.bfloat16)
    partial_out = jnp.einsum(
        "hqk,khd->qhd", global_probs, values_split, preferred_element_type=jnp.float32
    )
    global_out = lax.psum(partial_out, "ctx").astype(jnp.bfloat16)
    global_delta = jnp.sum(
        global_grad.astype(jnp.float32) * global_out.astype(jnp.float32), axis=-1
    ).T
    global_dprobs = jnp.einsum(
        "qhd,khd->hqk", global_grad, values_split, preferred_element_type=jnp.float32
    )
    global_dscores = (
        global_probs.astype(jnp.float32) * (global_dprobs - global_delta[..., None])
    ).astype(jnp.bfloat16)
    query_part = (
        jnp.einsum("hqk,khd->qhd", global_dscores, keys_split, preferred_element_type=jnp.float32)
        * scaling
    )
    key_from_global = (
        jnp.einsum("hqk,qhd->khd", global_dscores, global_query, preferred_element_type=jnp.float32)
        * scaling
    )
    value_from_global = jnp.einsum(
        "hqk,qhd->khd", global_probs, global_grad, preferred_element_type=jnp.float32
    )
    paired = jnp.stack([keys, values], axis=1)
    padded = extended(paired, (("ctx", 0),), BS)
    padded = padded.reshape(block_count + 2, BS, 2, head_count, DH)
    window = jnp.concatenate(
        [padded[start_block : start_block + block_count] for start_block in range(WIN)], axis=1
    )
    window = window.transpose(2, 3, 0, 1, 4)
    entry_blocks = (
        random_blocks.reshape(head_count, ctx_count, block_count, RAND)
        .transpose(1, 0, 2, 3)
        .reshape(ctx_count, entry_count)
    )
    owner_of = entry_blocks // block_count
    local_of = entry_blocks % block_count
    entry_ids = jnp.arange(entry_count, dtype=jnp.int32)
    head_of = entry_ids // (block_count * RAND)
    onehot = (owner_of[:, :, None] == jnp.arange(ctx_count, dtype=jnp.int32)[None, None, :]).astype(
        jnp.int32
    )
    before = jnp.cumsum(onehot, axis=1) - onehot
    rank_of = jnp.sum(before * onehot, axis=2)
    slot_hit = (owner_of == own_index)[:, :, None] & (
        rank_of[:, :, None] == jnp.arange(capacity, dtype=jnp.int32)[None, None, :]
    )
    send_index = jnp.sum(
        jnp.where(slot_hit, (local_of * head_count + head_of[None, :])[:, :, None], 0), axis=1
    )
    my_owner = lax.dynamic_index_in_dim(owner_of, own_index, axis=0, keepdims=False)
    my_rank = lax.dynamic_index_in_dim(rank_of, own_index, axis=0, keepdims=False)
    my_place = my_owner * capacity + my_rank
    masked_grad = (
        out_grad.reshape(block_count, BS, features) * keep_rows.astype(jnp.bfloat16)[:, None, None]
    ).reshape(local_rows, features)

    def to_table(tensor):
        return (
            tensor.reshape(block_count, BS, head_count, DH)
            .transpose(0, 2, 1, 3)
            .reshape(block_count * head_count, BS, DH)
        )

    send_keys = picked(to_table(keys), send_index)
    send_values = picked(to_table(values), send_index)
    got_keys, got_values = (
        lax.all_to_all(send_keys, "ctx", split_axis=0, concat_axis=0, tiled=True),
        lax.all_to_all(send_values, "ctx", split_axis=0, concat_axis=0, tiled=True),
    )
    random_keys = picked(got_keys.reshape(ctx_count * capacity, BS, DH), my_place).reshape(
        head_count, block_count, RAND * BS, DH
    )
    random_values = picked(got_values.reshape(ctx_count * capacity, BS, DH), my_place).reshape(
        head_count, block_count, RAND * BS, DH
    )
    query_heads = queries.reshape(block_count, BS, head_count, DH).transpose(2, 0, 1, 3)
    grad_heads = masked_grad.reshape(block_count, BS, head_count, DH).transpose(2, 0, 1, 3)
    global_key_heads = global_key.transpose(1, 0, 2)
    global_value_heads = global_value.transpose(1, 0, 2)
    window_cols = WIN * BS
    random_end = (WIN + RAND) * BS

    def head_work(inputs):
        (
            query_head,
            grad_head,
            win_keys,
            win_values,
            rand_keys,
            rand_values,
            glob_keys,
            glob_values,
        ) = inputs
        key_list = jnp.concatenate(
            [
                win_keys,
                rand_keys,
                jnp.broadcast_to(glob_keys[None], (block_count,) + glob_keys.shape),
            ],
            axis=1,
        )
        value_list = jnp.concatenate(
            [
                win_values,
                rand_values,
                jnp.broadcast_to(glob_values[None], (block_count,) + glob_values.shape),
            ],
            axis=1,
        )
        output, logsum, deltas, probs, dscores, dquery = sparse_rows(
            query_head, key_list, value_list, grad_head, scaling
        )
        win_dk = (
            jnp.einsum(
                "nqk,nqd->nkd",
                dscores[:, :, :window_cols],
                query_head,
                preferred_element_type=jnp.float32,
            )
            * scaling
        )
        win_dv = jnp.einsum(
            "nqk,nqd->nkd", probs[:, :, :window_cols], grad_head, preferred_element_type=jnp.float32
        )
        glob_dk = (
            jnp.einsum(
                "nqk,nqd->kd",
                dscores[:, :, random_end:],
                query_head,
                preferred_element_type=jnp.float32,
            )
            * scaling
        )
        glob_dv = jnp.einsum(
            "nqk,nqd->kd", probs[:, :, random_end:], grad_head, preferred_element_type=jnp.float32
        )
        win_dk = win_dk.reshape(block_count, WIN, BS, DH)
        win_dv = win_dv.reshape(block_count, WIN, BS, DH)
        ext_dk = sum(
            (
                jnp.pad(win_dk[:, shift_by], ((shift_by, WIN - 1 - shift_by), (0, 0), (0, 0)))
                for shift_by in range(WIN)
            )
        )
        ext_dv = sum(
            (
                jnp.pad(win_dv[:, shift_by], ((shift_by, WIN - 1 - shift_by), (0, 0), (0, 0)))
                for shift_by in range(WIN)
            )
        )
        rand_dk = (
            jnp.einsum(
                "nqk,nqd->nkd",
                dscores[:, :, window_cols:random_end],
                query_head,
                preferred_element_type=jnp.float32,
            )
            * scaling
        )
        rand_dv = jnp.einsum(
            "nqk,nqd->nkd",
            probs[:, :, window_cols:random_end],
            grad_head,
            preferred_element_type=jnp.float32,
        )
        return (output, logsum, deltas, dquery, ext_dk, ext_dv, glob_dk, glob_dv, rand_dk, rand_dv)

    results = lax.map(
        head_work,
        (
            query_heads,
            grad_heads,
            window[0],
            window[1],
            random_keys,
            random_values,
            global_key_heads,
            global_value_heads,
        ),
    )
    output_heads, logsums, deltas, dquery_heads, ext_dk, ext_dv, glob_dk, glob_dv = results[:8]
    query_total, glob_dk_total, glob_dv_total = lax.psum((query_part, glob_dk, glob_dv), "ctx")
    rim_low = jnp.stack([ext_dk[:, 0], ext_dv[:, 0]], axis=0)
    rim_high = jnp.stack([ext_dk[:, block_count + 1], ext_dv[:, block_count + 1]], axis=0)
    from_next = from_behind(rim_low.astype(jnp.bfloat16), "ctx", -1).astype(rim_low.dtype)
    from_prev = from_behind(rim_high.astype(jnp.bfloat16), "ctx", 1).astype(rim_high.dtype)
    key_heads = ext_dk[:, 1 : block_count + 1]
    value_heads = ext_dv[:, 1 : block_count + 1]
    key_heads = key_heads.at[:, 0].add(from_prev[0]).at[:, block_count - 1].add(from_next[0])
    value_heads = value_heads.at[:, 0].add(from_prev[1]).at[:, block_count - 1].add(from_next[1])
    rand_dk = results[8].reshape(entry_count, BS, DH)
    rand_dv = results[9].reshape(entry_count, BS, DH)
    out_keys = (
        jnp.zeros((ctx_count * capacity, BS, DH), jnp.float32)
        .at[my_place]
        .set(rand_dk)
        .reshape(ctx_count, capacity, BS, DH)
    )
    out_values = (
        jnp.zeros((ctx_count * capacity, BS, DH), jnp.float32)
        .at[my_place]
        .set(rand_dv)
        .reshape(ctx_count, capacity, BS, DH)
    )
    back_keys, back_values = (
        lax.all_to_all(out_keys, "ctx", split_axis=0, concat_axis=0, tiled=True),
        lax.all_to_all(out_values, "ctx", split_axis=0, concat_axis=0, tiled=True),
    )
    back_keys = back_keys.reshape(ctx_count * capacity, BS, DH)
    back_values = back_values.reshape(ctx_count * capacity, BS, DH)
    flat_index = send_index.reshape(-1)
    table_keys = (
        jnp.zeros((block_count * head_count, BS, DH), jnp.float32).at[flat_index].add(back_keys)
    )
    table_values = (
        jnp.zeros((block_count * head_count, BS, DH), jnp.float32).at[flat_index].add(back_values)
    )
    key_heads = key_heads + table_keys.reshape(block_count, head_count, BS, DH).transpose(
        1, 0, 2, 3
    )
    value_heads = value_heads + table_values.reshape(block_count, head_count, BS, DH).transpose(
        1, 0, 2, 3
    )

    def place_global(tensor):
        return jnp.sum(global_hit[None, :, :, None, None] * tensor[:, None], axis=2)

    key_heads = key_heads + place_global(glob_dk_total.reshape(head_count, GLOBAL, BS, DH))
    value_heads = value_heads + place_global(glob_dv_total.reshape(head_count, GLOBAL, BS, DH))
    key_heads = key_heads + key_from_global.reshape(block_count, BS, head_count, DH).transpose(
        2, 0, 1, 3
    )
    value_heads = value_heads + value_from_global.reshape(
        block_count, BS, head_count, DH
    ).transpose(2, 0, 1, 3)
    query_heads_total = dquery_heads + place_global(
        query_total.reshape(GLOBAL, BS, head_count, DH).transpose(2, 0, 1, 3)
    )
    output_total = output_heads.astype(jnp.float32) * keep_rows[None, :, None, None]
    output_total = output_total + place_global(
        global_out.astype(jnp.float32).reshape(GLOBAL, BS, head_count, DH).transpose(2, 0, 1, 3)
    )

    def to_rows(tensor):
        return tensor.transpose(1, 2, 0, 3).reshape(local_rows, features).astype(jnp.bfloat16)

    return (
        to_rows(output_total),
        to_rows(query_heads_total),
        to_rows(key_heads),
        to_rows(value_heads),
    )


Q, K, V, G = range(4)
LOG2E = 1.4426950408889634
VMEM_LIMIT = 40 * 1024 * 1024
GROUP = 4


def peer(step):
    me = lax.axis_index("ctx")
    return (me // 2 + step // 2) % 2 * 2 + (me % 2 + step % 2) % 2


def heads_kernel(
    random_hbm,
    global_hbm,
    q_ref,
    k_ref,
    v_ref,
    g_ref,
    att_ref,
    dq_ref,
    dk_ref,
    dv_ref,
    inb,
    outb,
    probs_buf,
    att_buf,
    dk_acc,
    dv_acc,
    bias,
    k_t,
    v_t,
    own_in,
    own_out,
    in_send,
    in_recv,
    out_send,
    out_recv,
    relay,
    random_ref,
    global_ref,
    list_sem,
):
    n = GROUP
    me = lax.axis_index("ctx")
    rows = q_ref.shape[0]
    seq = n * rows
    blocks = seq // BS
    scaling = DH ** (-0.5)
    sources = (q_ref, k_ref, v_ref, g_ref)
    targets = (att_ref, dq_ref, dk_ref, dv_ref)

    def at_rows(device):
        return pl.ds(pl.multiple_of(device * rows, rows), rows)

    def at_head(device):
        return pl.ds(pl.multiple_of(device * DH, DH), DH)

    def in_copy(array, step, land):
        other = peer(step)
        return pltpu.make_async_remote_copy(
            src_ref=sources[array].at[:, at_head(other)],
            dst_ref=inb.at[array, at_rows(land)],
            send_sem=in_send.at[array, step - 1],
            recv_sem=in_recv.at[array, step - 1],
            device_id={"ctx": other},
            device_id_type=pl.DeviceIdType.MESH,
        )

    def out_copy(array, step, land):
        other = peer(step)
        return pltpu.make_async_remote_copy(
            src_ref=outb.at[array, at_rows(other)],
            dst_ref=targets[array].at[:, at_head(land)],
            send_sem=out_send.at[array, step - 1],
            recv_sem=out_recv.at[array, step - 1],
            device_id={"ctx": other},
            device_id_type=pl.DeviceIdType.MESH,
        )

    def own_copy_in(array):
        return pltpu.make_async_copy(
            sources[array].at[:, at_head(me)], inb.at[array, at_rows(me)], own_in.at[array]
        )

    def own_copy_out(array):
        return pltpu.make_async_copy(
            outb.at[array, at_rows(me)], targets[array].at[:, at_head(me)], own_out.at[array]
        )

    def arrived(array, step):
        if step == 0:
            own_copy_in(array).wait()
        else:
            in_copy(array, step, peer(step)).wait_recv()

    def leave(array, step):
        (own_copy_out(array) if step == 0 else out_copy(array, step, me)).start()

    barrier = pltpu.get_barrier_semaphore()
    for step in (2, 3):
        pl.semaphore_signal(
            barrier,
            inc=1,
            device_id={"ctx": peer(step)},
            device_id_type=pl.DeviceIdType.MESH,
        )
    random_copy = pltpu.make_async_copy(random_hbm, random_ref, list_sem.at[0])
    global_copy = pltpu.make_async_copy(global_hbm, global_ref, list_sem.at[1])
    random_copy.start()
    global_copy.start()
    for array in (K, V, Q, G):
        own_copy_in(array).start()
    pl.semaphore_wait(barrier, 2)
    for array in (K, V, Q, G):
        for step in (2, 3):
            in_copy(array, step, me).start()
    pl.semaphore_signal(
        relay, inc=1, device_id={"ctx": peer(2)}, device_id_type=pl.DeviceIdType.MESH
    )
    pl.semaphore_wait(relay, 1)
    for array in (K, V, Q, G):
        in_copy(array, 1, me).start()

    random_copy.wait()
    global_copy.wait()
    key_block = lax.broadcasted_iota(jnp.int32, (blocks, BS), 0)
    first, second = (global_ref[0], global_ref[1])
    per_device = rows // BS
    for block in range(blocks):
        query_block = jnp.full((blocks, BS), block, jnp.int32)
        named = [(block - 1) % blocks, block, (block + 1) % blocks]
        named += [random_ref[entry, me, block] for entry in range(RAND)]
        named += [first, second]
        count = sum((key_block == one).astype(jnp.int32) for one in named)
        is_global = (query_block == first) | (query_block == second)
        count = jnp.where(is_global, 1, count).astype(jnp.float32)
        level = jnp.where(count > 0.5, jnp.log2(jnp.maximum(count, 1.0)), -1e30)
        lanes = slice(block % per_device * BS, block % per_device * BS + BS)
        bias[block // per_device, :, lanes] = level

    contract_last = (((1,), (1,)), ((), ()))

    def weigh(step):
        arrived(Q, step)
        owner = peer(step)
        query = inb[Q, at_rows(owner)]
        scores = lax.dot_general(inb[K], query, contract_last, preferred_element_type=jnp.float32)
        scores = scores.reshape(blocks, BS, rows) * (scaling * LOG2E) + bias[owner][:, None, :]
        highest = jnp.max(scores, axis=(0, 1), keepdims=True)
        weights = jnp.exp2(scores - highest)
        total = jnp.sum(weights, axis=(0, 1), keepdims=True)
        probs = (weights * (1.0 / total)).reshape(seq, rows).astype(jnp.bfloat16)
        probs_buf[step] = probs

    def attend(step):
        att_t = jnp.dot(v_t[...], probs_buf[step], preferred_element_type=jnp.float32)
        att_t = att_t.astype(jnp.bfloat16).astype(jnp.float32)
        outb[0, at_rows(peer(step))] = att_t.T.astype(jnp.bfloat16)
        att_buf[step] = att_t
        leave(0, step)

    def differentiate(step):
        arrived(G, step)
        owner = peer(step)
        query = inb[Q, at_rows(owner)]
        grad = inb[G, at_rows(owner)]
        probs = probs_buf[step]
        delta = jnp.sum(grad.astype(jnp.float32).T * att_buf[step], axis=0, keepdims=True)
        dprobs = lax.dot_general(inb[V], grad, contract_last, preferred_element_type=jnp.float32)
        dscores = (probs.astype(jnp.float32) * (dprobs - delta)).astype(jnp.bfloat16)
        dq_t = jnp.dot(k_t[...], dscores, preferred_element_type=jnp.float32) * scaling
        outb[1, at_rows(owner)] = dq_t.T.astype(jnp.bfloat16)
        leave(1, step)
        dv = jnp.dot(probs, grad, preferred_element_type=jnp.float32)
        dk = jnp.dot(dscores, query, preferred_element_type=jnp.float32)
        dv_acc[...] = dv if step == 0 else dv_acc[...] + dv
        dk_acc[...] = dk if step == 0 else dk_acc[...] + dk

    for step in range(n):
        arrived(K, step)
    k_t[...] = inb[K].T
    weigh(0)
    weigh(1)
    for step in range(n):
        arrived(V, step)
    v_t[...] = inb[V].T
    attend(0)
    differentiate(0)
    for step in (2, 3):
        weigh(step)
        attend(step)
    attend(1)
    for step in (1, 2, 3):
        differentiate(step)

    outb[2] = (dk_acc[...] * scaling).astype(jnp.bfloat16)
    outb[3] = dv_acc[...].astype(jnp.bfloat16)
    for step in (2, 3, 1, 0):
        for array in (2, 3):
            leave(array, step)

    for array in range(4):
        own_copy_out(array).wait()
        for step in range(1, n):
            in_copy(array, step, me).wait_send()
            out_copy(array, step, me).wait_send()
            out_copy(array, step, peer(step)).wait_recv()


def place_kernel(*refs):
    copies = [
        pltpu.make_async_copy(refs[array], refs[4 + array], refs[8].at[array])
        for array in range(4)
    ]
    for copy in copies:
        copy.start()
    for copy in copies:
        copy.wait()


def by_heads(queries, keys, values, out_grad, random_blocks, global_blocks):
    n = GROUP
    rows, features = queries.shape
    seq = n * rows
    blocks = seq // BS
    anywhere = pl.BlockSpec(memory_space=pl.ANY)
    results = pl.pallas_call(
        heads_kernel,
        out_shape=[jax.ShapeDtypeStruct((rows, features), jnp.bfloat16)] * 4,
        in_specs=[anywhere] * 6,
        out_specs=[anywhere] * 4,
        scratch_shapes=[
            pltpu.VMEM((4, seq, DH), jnp.bfloat16),
            pltpu.VMEM((4, seq, DH), jnp.bfloat16),
            pltpu.VMEM((n, seq, rows), jnp.bfloat16),
            pltpu.VMEM((n, DH, rows), jnp.float32),
            pltpu.VMEM((seq, DH), jnp.float32),
            pltpu.VMEM((seq, DH), jnp.float32),
            pltpu.VMEM((n, blocks, rows), jnp.float32),
            pltpu.VMEM((DH, seq), jnp.bfloat16),
            pltpu.VMEM((DH, seq), jnp.bfloat16),
            pltpu.SemaphoreType.DMA((4,)),
            pltpu.SemaphoreType.DMA((4,)),
            pltpu.SemaphoreType.DMA((4, n - 1)),
            pltpu.SemaphoreType.DMA((4, n - 1)),
            pltpu.SemaphoreType.DMA((4, n - 1)),
            pltpu.SemaphoreType.DMA((4, n - 1)),
            pltpu.SemaphoreType.REGULAR,
            pltpu.SMEM((RAND, n, blocks), jnp.int32),
            pltpu.SMEM((GLOBAL,), jnp.int32),
            pltpu.SemaphoreType.DMA((2,)),
        ],
        compiler_params=pltpu.CompilerParams(
            collective_id=0, has_side_effects=True, vmem_limit_bytes=VMEM_LIMIT
        ),
    )(
        *(
            pltpu.with_memory_space_constraint(array, pltpu.HBM)
            for array in (
                random_blocks.transpose(2, 0, 1),
                global_blocks,
                queries,
                keys,
                values,
                out_grad,
            )
        )
    )
    return pl.pallas_call(
        place_kernel,
        out_shape=[jax.ShapeDtypeStruct((rows, features), jnp.bfloat16)] * 4,
        in_specs=[anywhere] * 4,
        out_specs=[anywhere] * 4,
        scratch_shapes=[pltpu.SemaphoreType.DMA((4,))],
        compiler_params=pltpu.CompilerParams(vmem_limit_bytes=VMEM_LIMIT),
    )(*results)


def solution(mesh):
    in_specs = (
        P(("dp", "ctx"), "head"),
        P(("dp", "ctx"), "head"),
        P(("dp", "ctx"), "head"),
        P(("dp", "ctx"), "head"),
        P(("dp", "head"), None, None),
        P("dp"),
    )
    out_specs = (
        P(("dp", "ctx"), "head"),
        P(("dp", "ctx"), "head"),
        P(("dp", "ctx"), "head"),
        P(("dp", "ctx"), "head"),
    )
    ctx_count = mesh.shape["ctx"]

    def body(queries, *rest):
        heads = queries.shape[1] // DH
        if heads == ctx_count == GROUP:
            return by_heads(queries, *rest)
        return on_device(queries, *rest)

    return jax.shard_map(
        body, mesh=mesh, in_specs=in_specs, out_specs=out_specs, check_vma=False
    )
```

```python
import jax
import jax.numpy as jnp
from jax import lax
from jax.experimental import pallas as pl
from jax.experimental.pallas import tpu as pltpu
from jax.sharding import PartitionSpec as P

DH = 128
BS = 128
WIN = 3
RAND = 3
GLOBAL = 2


def broadcast(value, axis, source):
    kept = jnp.where(lax.axis_index(axis) == source, value, 0).astype(value.dtype)
    return lax.psum(kept, axis)


def merged(part, axis, combine):
    gathered = jax.tree.map(lambda a: lax.all_gather(a, axis), part)

    def take(source):
        return jax.tree.map(lambda a: lax.dynamic_index_in_dim(a, source, 0, False), gathered)

    return lax.fori_loop(
        1, lax.axis_size(axis), lambda source, state: combine(state, take(source)), take(0)
    )


def extended(value, sides, width):
    for axis, dim in sides:
        size, length = (lax.axis_size(axis), value.shape[dim])
        up = [(i, (i + 1) % size) for i in range(size)]
        down = [(j, i) for i, j in up]
        last = lax.slice_in_dim(value, length - width, length, axis=dim)
        first = lax.slice_in_dim(value, 0, width, axis=dim)
        before = lax.ppermute(last, axis, up)
        after = lax.ppermute(first, axis, down)
        value = jnp.concatenate([before, value, after], axis=dim)
    return value


def from_behind(value, axis, by):
    length = lax.axis_size(axis)
    return lax.ppermute(value, axis, [(i, (i + by) % length) for i in range(length)])


def picked(table, index):
    rows = lax.map(
        lambda one: lax.dynamic_index_in_dim(table, one, 0, False), index.reshape(-1)
    )
    return rows.reshape(index.shape + table.shape[1:])


def combine_stats(first_pair, second_pair):
    highest = jnp.maximum(first_pair[0], second_pair[0])
    summed = first_pair[1] * jnp.exp(first_pair[0] - highest) + second_pair[1] * jnp.exp(
        second_pair[0] - highest
    )
    return (highest, summed)


def sparse_rows(query_head, key_list, value_list, grad_head, scaling):
    scores = (
        jnp.einsum("nqd,nkd->nqk", query_head, key_list, preferred_element_type=jnp.float32)
        * scaling
    )
    highest = jnp.max(scores, axis=-1, keepdims=True)
    logsum = highest + jnp.log(jnp.sum(jnp.exp(scores - highest), axis=-1, keepdims=True))
    probs = jnp.exp(scores - logsum).astype(jnp.bfloat16)
    output = jnp.einsum(
        "nqk,nkd->nqd", probs, value_list, preferred_element_type=jnp.float32
    ).astype(jnp.bfloat16)
    deltas = jnp.sum(
        grad_head.astype(jnp.float32) * output.astype(jnp.float32), axis=-1, keepdims=True
    )
    dprobs = jnp.einsum("nqd,nkd->nqk", grad_head, value_list, preferred_element_type=jnp.float32)
    dscores = (probs.astype(jnp.float32) * (dprobs - deltas)).astype(jnp.bfloat16)
    dquery = (
        jnp.einsum("nqk,nkd->nqd", dscores, key_list, preferred_element_type=jnp.float32) * scaling
    )
    return (output, logsum[..., 0], deltas[..., 0], probs, dscores, dquery)


def on_device(queries, keys, values, out_grad, random_blocks, global_blocks):
    ctx_count = lax.axis_size("ctx")
    own_index = lax.axis_index("ctx")
    head_count = random_blocks.shape[0]
    local_rows = queries.shape[0]
    block_count = local_rows // BS
    features = queries.shape[1]
    scaling = DH ** (-0.5)
    entry_count = head_count * block_count * RAND
    capacity = (entry_count + ctx_count - 1) // ctx_count
    block_ids = own_index * block_count + jnp.arange(block_count, dtype=jnp.int32)
    global_hit = (block_ids[:, None] == global_blocks[None, :]).astype(jnp.float32)
    keep_rows = 1.0 - jnp.sum(global_hit, axis=1)
    stacked = jnp.stack([queries, keys, values, out_grad], axis=0)
    received = []
    for position in range(GLOBAL):
        holder_index = global_blocks[position] // block_count
        offset = global_blocks[position] % block_count * BS
        block_piece = lax.dynamic_slice_in_dim(stacked, offset, BS, axis=1)
        received.append(broadcast(block_piece, "ctx", holder_index))
    global_data = jnp.stack(received, axis=1).reshape(4, GLOBAL * BS, head_count, DH)
    global_query = global_data[0]
    global_key = global_data[1]
    global_value = global_data[2]
    global_grad = global_data[3]
    keys_split = keys.reshape(local_rows, head_count, DH)
    values_split = values.reshape(local_rows, head_count, DH)
    global_scores = (
        jnp.einsum("qhd,khd->hqk", global_query, keys_split, preferred_element_type=jnp.float32)
        * scaling
    )
    local_max = jnp.max(global_scores, axis=-1)
    local_sum = jnp.sum(jnp.exp(global_scores - local_max[..., None]), axis=-1)
    merged_max, merged_sum = merged((local_max, local_sum), "ctx", combine_stats)
    global_lse = merged_max + jnp.log(merged_sum)
    global_probs = jnp.exp(global_scores - global_lse[..., None]).astype(jnp.bfloat16)
    partial_out = jnp.einsum(
        "hqk,khd->qhd", global_probs, values_split, preferred_element_type=jnp.float32
    )
    global_out = lax.psum(partial_out, "ctx").astype(jnp.bfloat16)
    global_delta = jnp.sum(
        global_grad.astype(jnp.float32) * global_out.astype(jnp.float32), axis=-1
    ).T
    global_dprobs = jnp.einsum(
        "qhd,khd->hqk", global_grad, values_split, preferred_element_type=jnp.float32
    )
    global_dscores = (
        global_probs.astype(jnp.float32) * (global_dprobs - global_delta[..., None])
    ).astype(jnp.bfloat16)
    query_part = (
        jnp.einsum("hqk,khd->qhd", global_dscores, keys_split, preferred_element_type=jnp.float32)
        * scaling
    )
    key_from_global = (
        jnp.einsum("hqk,qhd->khd", global_dscores, global_query, preferred_element_type=jnp.float32)
        * scaling
    )
    value_from_global = jnp.einsum(
        "hqk,qhd->khd", global_probs, global_grad, preferred_element_type=jnp.float32
    )
    paired = jnp.stack([keys, values], axis=1)
    padded = extended(paired, (("ctx", 0),), BS)
    padded = padded.reshape(block_count + 2, BS, 2, head_count, DH)
    window = jnp.concatenate(
        [padded[start_block : start_block + block_count] for start_block in range(WIN)], axis=1
    )
    window = window.transpose(2, 3, 0, 1, 4)
    entry_blocks = (
        random_blocks.reshape(head_count, ctx_count, block_count, RAND)
        .transpose(1, 0, 2, 3)
        .reshape(ctx_count, entry_count)
    )
    owner_of = entry_blocks // block_count
    local_of = entry_blocks % block_count
    entry_ids = jnp.arange(entry_count, dtype=jnp.int32)
    head_of = entry_ids // (block_count * RAND)
    onehot = (owner_of[:, :, None] == jnp.arange(ctx_count, dtype=jnp.int32)[None, None, :]).astype(
        jnp.int32
    )
    before = jnp.cumsum(onehot, axis=1) - onehot
    rank_of = jnp.sum(before * onehot, axis=2)
    slot_hit = (owner_of == own_index)[:, :, None] & (
        rank_of[:, :, None] == jnp.arange(capacity, dtype=jnp.int32)[None, None, :]
    )
    send_index = jnp.sum(
        jnp.where(slot_hit, (local_of * head_count + head_of[None, :])[:, :, None], 0), axis=1
    )
    my_owner = lax.dynamic_index_in_dim(owner_of, own_index, axis=0, keepdims=False)
    my_rank = lax.dynamic_index_in_dim(rank_of, own_index, axis=0, keepdims=False)
    my_place = my_owner * capacity + my_rank
    masked_grad = (
        out_grad.reshape(block_count, BS, features) * keep_rows.astype(jnp.bfloat16)[:, None, None]
    ).reshape(local_rows, features)

    def to_table(tensor):
        return (
            tensor.reshape(block_count, BS, head_count, DH)
            .transpose(0, 2, 1, 3)
            .reshape(block_count * head_count, BS, DH)
        )

    send_keys = picked(to_table(keys), send_index)
    send_values = picked(to_table(values), send_index)
    got_keys, got_values = (
        lax.all_to_all(send_keys, "ctx", split_axis=0, concat_axis=0, tiled=True),
        lax.all_to_all(send_values, "ctx", split_axis=0, concat_axis=0, tiled=True),
    )
    random_keys = picked(got_keys.reshape(ctx_count * capacity, BS, DH), my_place).reshape(
        head_count, block_count, RAND * BS, DH
    )
    random_values = picked(got_values.reshape(ctx_count * capacity, BS, DH), my_place).reshape(
        head_count, block_count, RAND * BS, DH
    )
    query_heads = queries.reshape(block_count, BS, head_count, DH).transpose(2, 0, 1, 3)
    grad_heads = masked_grad.reshape(block_count, BS, head_count, DH).transpose(2, 0, 1, 3)
    global_key_heads = global_key.transpose(1, 0, 2)
    global_value_heads = global_value.transpose(1, 0, 2)
    window_cols = WIN * BS
    random_end = (WIN + RAND) * BS

    def head_work(inputs):
        (
            query_head,
            grad_head,
            win_keys,
            win_values,
            rand_keys,
            rand_values,
            glob_keys,
            glob_values,
        ) = inputs
        key_list = jnp.concatenate(
            [
                win_keys,
                rand_keys,
                jnp.broadcast_to(glob_keys[None], (block_count,) + glob_keys.shape),
            ],
            axis=1,
        )
        value_list = jnp.concatenate(
            [
                win_values,
                rand_values,
                jnp.broadcast_to(glob_values[None], (block_count,) + glob_values.shape),
            ],
            axis=1,
        )
        output, logsum, deltas, probs, dscores, dquery = sparse_rows(
            query_head, key_list, value_list, grad_head, scaling
        )
        win_dk = (
            jnp.einsum(
                "nqk,nqd->nkd",
                dscores[:, :, :window_cols],
                query_head,
                preferred_element_type=jnp.float32,
            )
            * scaling
        )
        win_dv = jnp.einsum(
            "nqk,nqd->nkd", probs[:, :, :window_cols], grad_head, preferred_element_type=jnp.float32
        )
        glob_dk = (
            jnp.einsum(
                "nqk,nqd->kd",
                dscores[:, :, random_end:],
                query_head,
                preferred_element_type=jnp.float32,
            )
            * scaling
        )
        glob_dv = jnp.einsum(
            "nqk,nqd->kd", probs[:, :, random_end:], grad_head, preferred_element_type=jnp.float32
        )
        win_dk = win_dk.reshape(block_count, WIN, BS, DH)
        win_dv = win_dv.reshape(block_count, WIN, BS, DH)
        ext_dk = sum(
            (
                jnp.pad(win_dk[:, shift_by], ((shift_by, WIN - 1 - shift_by), (0, 0), (0, 0)))
                for shift_by in range(WIN)
            )
        )
        ext_dv = sum(
            (
                jnp.pad(win_dv[:, shift_by], ((shift_by, WIN - 1 - shift_by), (0, 0), (0, 0)))
                for shift_by in range(WIN)
            )
        )
        rand_dk = (
            jnp.einsum(
                "nqk,nqd->nkd",
                dscores[:, :, window_cols:random_end],
                query_head,
                preferred_element_type=jnp.float32,
            )
            * scaling
        )
        rand_dv = jnp.einsum(
            "nqk,nqd->nkd",
            probs[:, :, window_cols:random_end],
            grad_head,
            preferred_element_type=jnp.float32,
        )
        return (output, logsum, deltas, dquery, ext_dk, ext_dv, glob_dk, glob_dv, rand_dk, rand_dv)

    results = lax.map(
        head_work,
        (
            query_heads,
            grad_heads,
            window[0],
            window[1],
            random_keys,
            random_values,
            global_key_heads,
            global_value_heads,
        ),
    )
    output_heads, logsums, deltas, dquery_heads, ext_dk, ext_dv, glob_dk, glob_dv = results[:8]
    query_total, glob_dk_total, glob_dv_total = lax.psum((query_part, glob_dk, glob_dv), "ctx")
    rim_low = jnp.stack([ext_dk[:, 0], ext_dv[:, 0]], axis=0)
    rim_high = jnp.stack([ext_dk[:, block_count + 1], ext_dv[:, block_count + 1]], axis=0)
    from_next = from_behind(rim_low.astype(jnp.bfloat16), "ctx", -1).astype(rim_low.dtype)
    from_prev = from_behind(rim_high.astype(jnp.bfloat16), "ctx", 1).astype(rim_high.dtype)
    key_heads = ext_dk[:, 1 : block_count + 1]
    value_heads = ext_dv[:, 1 : block_count + 1]
    key_heads = key_heads.at[:, 0].add(from_prev[0]).at[:, block_count - 1].add(from_next[0])
    value_heads = value_heads.at[:, 0].add(from_prev[1]).at[:, block_count - 1].add(from_next[1])
    rand_dk = results[8].reshape(entry_count, BS, DH)
    rand_dv = results[9].reshape(entry_count, BS, DH)
    out_keys = (
        jnp.zeros((ctx_count * capacity, BS, DH), jnp.float32)
        .at[my_place]
        .set(rand_dk)
        .reshape(ctx_count, capacity, BS, DH)
    )
    out_values = (
        jnp.zeros((ctx_count * capacity, BS, DH), jnp.float32)
        .at[my_place]
        .set(rand_dv)
        .reshape(ctx_count, capacity, BS, DH)
    )
    back_keys, back_values = (
        lax.all_to_all(out_keys, "ctx", split_axis=0, concat_axis=0, tiled=True),
        lax.all_to_all(out_values, "ctx", split_axis=0, concat_axis=0, tiled=True),
    )
    back_keys = back_keys.reshape(ctx_count * capacity, BS, DH)
    back_values = back_values.reshape(ctx_count * capacity, BS, DH)
    flat_index = send_index.reshape(-1)
    table_keys = (
        jnp.zeros((block_count * head_count, BS, DH), jnp.float32).at[flat_index].add(back_keys)
    )
    table_values = (
        jnp.zeros((block_count * head_count, BS, DH), jnp.float32).at[flat_index].add(back_values)
    )
    key_heads = key_heads + table_keys.reshape(block_count, head_count, BS, DH).transpose(
        1, 0, 2, 3
    )
    value_heads = value_heads + table_values.reshape(block_count, head_count, BS, DH).transpose(
        1, 0, 2, 3
    )

    def place_global(tensor):
        return jnp.sum(global_hit[None, :, :, None, None] * tensor[:, None], axis=2)

    key_heads = key_heads + place_global(glob_dk_total.reshape(head_count, GLOBAL, BS, DH))
    value_heads = value_heads + place_global(glob_dv_total.reshape(head_count, GLOBAL, BS, DH))
    key_heads = key_heads + key_from_global.reshape(block_count, BS, head_count, DH).transpose(
        2, 0, 1, 3
    )
    value_heads = value_heads + value_from_global.reshape(
        block_count, BS, head_count, DH
    ).transpose(2, 0, 1, 3)
    query_heads_total = dquery_heads + place_global(
        query_total.reshape(GLOBAL, BS, head_count, DH).transpose(2, 0, 1, 3)
    )
    output_total = output_heads.astype(jnp.float32) * keep_rows[None, :, None, None]
    output_total = output_total + place_global(
        global_out.astype(jnp.float32).reshape(GLOBAL, BS, head_count, DH).transpose(2, 0, 1, 3)
    )

    def to_rows(tensor):
        return tensor.transpose(1, 2, 0, 3).reshape(local_rows, features).astype(jnp.bfloat16)

    return (
        to_rows(output_total),
        to_rows(query_heads_total),
        to_rows(key_heads),
        to_rows(value_heads),
    )


Q, K, V, G = range(4)
LOG2E = 1.4426950408889634
VMEM_LIMIT = 40 * 1024 * 1024
GROUP = 4
TILE_W = 256
TILE_D = 128


def peer(step):
    me = lax.axis_index("ctx")
    return (me // 2 + step // 2) % 2 * 2 + (me % 2 + step % 2) % 2


def heads_kernel(
    random_hbm,
    global_hbm,
    q_ref,
    k_ref,
    v_ref,
    g_ref,
    att_ref,
    dq_ref,
    dk_ref,
    dv_ref,
    inb,
    outb,
    scores_buf,
    weights_buf,
    dscores_buf,
    share,
    att_buf,
    dk_acc,
    dv_acc,
    bias,
    k_t,
    v_t,
    own_in,
    own_out,
    in_send,
    in_recv,
    out_send,
    out_recv,
    relay,
    random_ref,
    global_ref,
    list_sem,
):
    n = GROUP
    me = lax.axis_index("ctx")
    rows = q_ref.shape[0]
    seq = n * rows
    blocks = seq // BS
    scaling = DH ** (-0.5)
    sources = (q_ref, k_ref, v_ref, g_ref)
    targets = (att_ref, dq_ref, dk_ref, dv_ref)

    def at_rows(device):
        return pl.ds(pl.multiple_of(device * rows, rows), rows)

    def at_head(device):
        return pl.ds(pl.multiple_of(device * DH, DH), DH)

    def in_copy(array, step, land):
        other = peer(step)
        return pltpu.make_async_remote_copy(
            src_ref=sources[array].at[:, at_head(other)],
            dst_ref=inb.at[array, at_rows(land)],
            send_sem=in_send.at[array, step - 1],
            recv_sem=in_recv.at[array, step - 1],
            device_id={"ctx": other},
            device_id_type=pl.DeviceIdType.MESH,
        )

    def out_copy(array, step, land):
        other = peer(step)
        return pltpu.make_async_remote_copy(
            src_ref=outb.at[array, at_rows(other)],
            dst_ref=targets[array].at[:, at_head(land)],
            send_sem=out_send.at[array, step - 1],
            recv_sem=out_recv.at[array, step - 1],
            device_id={"ctx": other},
            device_id_type=pl.DeviceIdType.MESH,
        )

    def own_copy_in(array):
        return pltpu.make_async_copy(
            sources[array].at[:, at_head(me)], inb.at[array, at_rows(me)], own_in.at[array]
        )

    def own_copy_out(array):
        return pltpu.make_async_copy(
            outb.at[array, at_rows(me)], targets[array].at[:, at_head(me)], own_out.at[array]
        )

    def arrived(array, step):
        if step == 0:
            own_copy_in(array).wait()
        else:
            in_copy(array, step, peer(step)).wait_recv()

    def leave(array, step):
        (own_copy_out(array) if step == 0 else out_copy(array, step, me)).start()

    barrier = pltpu.get_barrier_semaphore()

    def greet(semaphore, step):
        pl.semaphore_signal(
            semaphore, inc=1, device_id={"ctx": peer(step)}, device_id_type=pl.DeviceIdType.MESH
        )

    greet(barrier, 2)
    greet(barrier, 3)
    pl.semaphore_wait(barrier, 2)
    for array in (K, V, Q, G):
        for step in (2, 3):
            in_copy(array, step, me).start()
    greet(relay, 2)
    random_copy = pltpu.make_async_copy(random_hbm, random_ref, list_sem.at[0])
    global_copy = pltpu.make_async_copy(global_hbm, global_ref, list_sem.at[1])
    random_copy.start()
    global_copy.start()
    for array in (K, V, Q, G):
        own_copy_in(array).start()
    pl.semaphore_wait(relay, 1)
    for array in (K, V, Q, G):
        in_copy(array, 1, me).start()

    random_copy.wait()
    global_copy.wait()
    key_block = lax.broadcasted_iota(jnp.int32, (blocks, BS), 0)
    first, second = (global_ref[0], global_ref[1])
    per_device = rows // BS
    for block in range(blocks):
        query_block = jnp.full((blocks, BS), block, jnp.int32)
        named = [(block - 1) % blocks, block, (block + 1) % blocks]
        named += [random_ref[entry, me, block] for entry in range(RAND)]
        named += [first, second]
        count = sum((key_block == one).astype(jnp.int32) for one in named)
        is_global = (query_block == first) | (query_block == second)
        count = jnp.where(is_global, 1, count).astype(jnp.float32)
        level = jnp.where(count > 0.5, jnp.log2(jnp.maximum(count, 1.0)), -1e30)
        lanes = slice(block % per_device * BS, block % per_device * BS + BS)
        bias[block // per_device, :, lanes] = level

    contract_last = (((1,), (1,)), ((), ()))

    def folded(tile, combine):
        return combine(tile.reshape(-1, 8, rows), axis=0)

    def weigh(step):
        arrived(Q, step)
        owner = peer(step)
        query = inb[Q, at_rows(owner)]
        highest = jnp.full((8, rows), -3e38, jnp.float32)
        for start in range(0, seq, TILE_W):
            part = slice(start, start + TILE_W)
            scores = lax.dot_general(
                inb[K, part], query, contract_last, preferred_element_type=jnp.float32
            )
            level = bias[owner, start // BS : (start + TILE_W) // BS]
            scores = (
                scores.reshape(-1, BS, rows) * (scaling * LOG2E) + level[:, None, :]
            ).reshape(TILE_W, rows)
            scores_buf[part] = scores
            highest = jnp.maximum(highest, folded(scores, jnp.max))
        highest = jnp.max(highest, axis=0, keepdims=True)
        total = jnp.zeros((8, rows), jnp.float32)
        for start in range(0, seq, TILE_W):
            part = slice(start, start + TILE_W)
            weights = jnp.exp2(scores_buf[part] - highest)
            total = total + folded(weights, jnp.sum)
            weights_buf[step, part] = weights.astype(jnp.bfloat16)
        share[step] = 1.0 / jnp.sum(total, axis=0, keepdims=True)

    def attend(step):
        att_t = jnp.dot(v_t[...], weights_buf[step], preferred_element_type=jnp.float32)
        att_t = (att_t * share[step]).astype(jnp.bfloat16).astype(jnp.float32)
        outb[0, at_rows(peer(step))] = att_t.T.astype(jnp.bfloat16)
        att_buf[step] = att_t
        leave(0, step)

    def differentiate(step, opening):
        arrived(G, step)
        owner = peer(step)
        query_t = inb[Q, at_rows(owner)].astype(jnp.float32).T
        grad = inb[G, at_rows(owner)]
        grad_t = grad.astype(jnp.float32).T
        delta = jnp.sum(grad_t * att_buf[step], axis=0, keepdims=True)
        for start in range(0, seq, TILE_D):
            part = slice(start, start + TILE_D)
            dprobs = lax.dot_general(
                inb[V, part], grad, contract_last, preferred_element_type=jnp.float32
            )
            weights = weights_buf[step, part].astype(jnp.float32)
            dscores_buf[part] = (weights * (dprobs - delta)).astype(jnp.bfloat16)
        dq_t = jnp.dot(k_t[...], dscores_buf[...], preferred_element_type=jnp.float32)
        dq_t = dq_t * (share[step] * scaling)
        outb[1, at_rows(owner)] = dq_t.T.astype(jnp.bfloat16)
        leave(1, step)
        grad_share = (grad_t * share[step]).astype(jnp.bfloat16)
        query_share = (query_t * share[step]).astype(jnp.bfloat16)
        dv = lax.dot_general(
            weights_buf[step], grad_share, contract_last, preferred_element_type=jnp.float32
        )
        dk = lax.dot_general(
            dscores_buf[...], query_share, contract_last, preferred_element_type=jnp.float32
        )
        dv_acc[...] = dv if opening else dv_acc[...] + dv
        dk_acc[...] = dk if opening else dk_acc[...] + dk

    for step in range(n):
        arrived(K, step)
    k_t[...] = inb[K].T
    weigh(0)
    weigh(1)
    for step in range(n):
        arrived(V, step)
    v_t[...] = inb[V].T
    attend(0)
    differentiate(0, True)
    weigh(2)
    attend(2)
    weigh(3)
    attend(3)
    differentiate(2, False)
    attend(1)
    differentiate(1, False)
    differentiate(3, False)

    outb[2] = (dk_acc[...] * scaling).astype(jnp.bfloat16)
    outb[3] = dv_acc[...].astype(jnp.bfloat16)
    for step in (2, 3, 1, 0):
        for array in (2, 3):
            leave(array, step)

    for array in range(4):
        own_copy_out(array).wait()
        for step in range(1, n):
            in_copy(array, step, me).wait_send()
            out_copy(array, step, me).wait_send()
            out_copy(array, step, peer(step)).wait_recv()


def place_kernel(*refs):
    copies = [
        pltpu.make_async_copy(refs[array], refs[4 + array], refs[8].at[array])
        for array in range(4)
    ]
    for copy in copies:
        copy.start()
    for copy in copies:
        copy.wait()


def by_heads(queries, keys, values, out_grad, random_blocks, global_blocks):
    n = GROUP
    rows, features = queries.shape
    seq = n * rows
    blocks = seq // BS
    anywhere = pl.BlockSpec(memory_space=pl.ANY)
    results = pl.pallas_call(
        heads_kernel,
        out_shape=[jax.ShapeDtypeStruct((rows, features), jnp.bfloat16)] * 4,
        in_specs=[anywhere] * 6,
        out_specs=[anywhere] * 4,
        scratch_shapes=[
            pltpu.VMEM((4, seq, DH), jnp.bfloat16),
            pltpu.VMEM((4, seq, DH), jnp.bfloat16),
            pltpu.VMEM((seq, rows), jnp.float32),
            pltpu.VMEM((n, seq, rows), jnp.bfloat16),
            pltpu.VMEM((seq, rows), jnp.bfloat16),
            pltpu.VMEM((n, 1, rows), jnp.float32),
            pltpu.VMEM((n, DH, rows), jnp.float32),
            pltpu.VMEM((seq, DH), jnp.float32),
            pltpu.VMEM((seq, DH), jnp.float32),
            pltpu.VMEM((n, blocks, rows), jnp.float32),
            pltpu.VMEM((DH, seq), jnp.bfloat16),
            pltpu.VMEM((DH, seq), jnp.bfloat16),
            pltpu.SemaphoreType.DMA((4,)),
            pltpu.SemaphoreType.DMA((4,)),
            pltpu.SemaphoreType.DMA((4, n - 1)),
            pltpu.SemaphoreType.DMA((4, n - 1)),
            pltpu.SemaphoreType.DMA((4, n - 1)),
            pltpu.SemaphoreType.DMA((4, n - 1)),
            pltpu.SemaphoreType.REGULAR,
            pltpu.SMEM((RAND, n, blocks), jnp.int32),
            pltpu.SMEM((GLOBAL,), jnp.int32),
            pltpu.SemaphoreType.DMA((2,)),
        ],
        compiler_params=pltpu.CompilerParams(
            collective_id=0, has_side_effects=True, vmem_limit_bytes=VMEM_LIMIT
        ),
    )(
        *(
            pltpu.with_memory_space_constraint(array, pltpu.HBM)
            for array in (
                random_blocks.transpose(2, 0, 1),
                global_blocks,
                queries,
                keys,
                values,
                out_grad,
            )
        )
    )
    return pl.pallas_call(
        place_kernel,
        out_shape=[jax.ShapeDtypeStruct((rows, features), jnp.bfloat16)] * 4,
        in_specs=[anywhere] * 4,
        out_specs=[anywhere] * 4,
        scratch_shapes=[pltpu.SemaphoreType.DMA((4,))],
        compiler_params=pltpu.CompilerParams(vmem_limit_bytes=VMEM_LIMIT),
    )(*results)


def solution(mesh):
    in_specs = (
        P(("dp", "ctx"), "head"),
        P(("dp", "ctx"), "head"),
        P(("dp", "ctx"), "head"),
        P(("dp", "ctx"), "head"),
        P(("dp", "head"), None, None),
        P("dp"),
    )
    out_specs = (
        P(("dp", "ctx"), "head"),
        P(("dp", "ctx"), "head"),
        P(("dp", "ctx"), "head"),
        P(("dp", "ctx"), "head"),
    )
    ctx_count = mesh.shape["ctx"]

    def body(queries, *rest):
        heads = queries.shape[1] // DH
        if heads == ctx_count == GROUP:
            return by_heads(queries, *rest)
        return on_device(queries, *rest)

    return jax.shard_map(
        body, mesh=mesh, in_specs=in_specs, out_specs=out_specs, check_vma=False
    )
```

```python
import jax
import jax.numpy as jnp
from jax import lax
from jax.experimental import pallas as pl
from jax.experimental.pallas import tpu as pltpu
from jax.sharding import PartitionSpec as P

DH = 128
BS = 128
WIN = 3
RAND = 3
GLOBAL = 2


def broadcast(value, axis, source):
    kept = jnp.where(lax.axis_index(axis) == source, value, 0).astype(value.dtype)
    return lax.psum(kept, axis)


def merged(part, axis, combine):
    gathered = jax.tree.map(lambda a: lax.all_gather(a, axis), part)

    def take(source):
        return jax.tree.map(lambda a: lax.dynamic_index_in_dim(a, source, 0, False), gathered)

    return lax.fori_loop(
        1, lax.axis_size(axis), lambda source, state: combine(state, take(source)), take(0)
    )


def extended(value, sides, width):
    for axis, dim in sides:
        size, length = (lax.axis_size(axis), value.shape[dim])
        up = [(i, (i + 1) % size) for i in range(size)]
        down = [(j, i) for i, j in up]
        last = lax.slice_in_dim(value, length - width, length, axis=dim)
        first = lax.slice_in_dim(value, 0, width, axis=dim)
        before = lax.ppermute(last, axis, up)
        after = lax.ppermute(first, axis, down)
        value = jnp.concatenate([before, value, after], axis=dim)
    return value


def from_behind(value, axis, by):
    length = lax.axis_size(axis)
    return lax.ppermute(value, axis, [(i, (i + by) % length) for i in range(length)])


def picked(table, index):
    rows = lax.map(
        lambda one: lax.dynamic_index_in_dim(table, one, 0, False), index.reshape(-1)
    )
    return rows.reshape(index.shape + table.shape[1:])


def combine_stats(first_pair, second_pair):
    highest = jnp.maximum(first_pair[0], second_pair[0])
    summed = first_pair[1] * jnp.exp(first_pair[0] - highest) + second_pair[1] * jnp.exp(
        second_pair[0] - highest
    )
    return (highest, summed)


def sparse_rows(query_head, key_list, value_list, grad_head, scaling):
    scores = (
        jnp.einsum("nqd,nkd->nqk", query_head, key_list, preferred_element_type=jnp.float32)
        * scaling
    )
    highest = jnp.max(scores, axis=-1, keepdims=True)
    logsum = highest + jnp.log(jnp.sum(jnp.exp(scores - highest), axis=-1, keepdims=True))
    probs = jnp.exp(scores - logsum).astype(jnp.bfloat16)
    output = jnp.einsum(
        "nqk,nkd->nqd", probs, value_list, preferred_element_type=jnp.float32
    ).astype(jnp.bfloat16)
    deltas = jnp.sum(
        grad_head.astype(jnp.float32) * output.astype(jnp.float32), axis=-1, keepdims=True
    )
    dprobs = jnp.einsum("nqd,nkd->nqk", grad_head, value_list, preferred_element_type=jnp.float32)
    dscores = (probs.astype(jnp.float32) * (dprobs - deltas)).astype(jnp.bfloat16)
    dquery = (
        jnp.einsum("nqk,nkd->nqd", dscores, key_list, preferred_element_type=jnp.float32) * scaling
    )
    return (output, logsum[..., 0], deltas[..., 0], probs, dscores, dquery)


def on_device(queries, keys, values, out_grad, random_blocks, global_blocks):
    ctx_count = lax.axis_size("ctx")
    own_index = lax.axis_index("ctx")
    head_count = random_blocks.shape[0]
    local_rows = queries.shape[0]
    block_count = local_rows // BS
    features = queries.shape[1]
    scaling = DH ** (-0.5)
    entry_count = head_count * block_count * RAND
    capacity = (entry_count + ctx_count - 1) // ctx_count
    block_ids = own_index * block_count + jnp.arange(block_count, dtype=jnp.int32)
    global_hit = (block_ids[:, None] == global_blocks[None, :]).astype(jnp.float32)
    keep_rows = 1.0 - jnp.sum(global_hit, axis=1)
    stacked = jnp.stack([queries, keys, values, out_grad], axis=0)
    received = []
    for position in range(GLOBAL):
        holder_index = global_blocks[position] // block_count
        offset = global_blocks[position] % block_count * BS
        block_piece = lax.dynamic_slice_in_dim(stacked, offset, BS, axis=1)
        received.append(broadcast(block_piece, "ctx", holder_index))
    global_data = jnp.stack(received, axis=1).reshape(4, GLOBAL * BS, head_count, DH)
    global_query = global_data[0]
    global_key = global_data[1]
    global_value = global_data[2]
    global_grad = global_data[3]
    keys_split = keys.reshape(local_rows, head_count, DH)
    values_split = values.reshape(local_rows, head_count, DH)
    global_scores = (
        jnp.einsum("qhd,khd->hqk", global_query, keys_split, preferred_element_type=jnp.float32)
        * scaling
    )
    local_max = jnp.max(global_scores, axis=-1)
    local_sum = jnp.sum(jnp.exp(global_scores - local_max[..., None]), axis=-1)
    merged_max, merged_sum = merged((local_max, local_sum), "ctx", combine_stats)
    global_lse = merged_max + jnp.log(merged_sum)
    global_probs = jnp.exp(global_scores - global_lse[..., None]).astype(jnp.bfloat16)
    partial_out = jnp.einsum(
        "hqk,khd->qhd", global_probs, values_split, preferred_element_type=jnp.float32
    )
    global_out = lax.psum(partial_out, "ctx").astype(jnp.bfloat16)
    global_delta = jnp.sum(
        global_grad.astype(jnp.float32) * global_out.astype(jnp.float32), axis=-1
    ).T
    global_dprobs = jnp.einsum(
        "qhd,khd->hqk", global_grad, values_split, preferred_element_type=jnp.float32
    )
    global_dscores = (
        global_probs.astype(jnp.float32) * (global_dprobs - global_delta[..., None])
    ).astype(jnp.bfloat16)
    query_part = (
        jnp.einsum("hqk,khd->qhd", global_dscores, keys_split, preferred_element_type=jnp.float32)
        * scaling
    )
    key_from_global = (
        jnp.einsum("hqk,qhd->khd", global_dscores, global_query, preferred_element_type=jnp.float32)
        * scaling
    )
    value_from_global = jnp.einsum(
        "hqk,qhd->khd", global_probs, global_grad, preferred_element_type=jnp.float32
    )
    paired = jnp.stack([keys, values], axis=1)
    padded = extended(paired, (("ctx", 0),), BS)
    padded = padded.reshape(block_count + 2, BS, 2, head_count, DH)
    window = jnp.concatenate(
        [padded[start_block : start_block + block_count] for start_block in range(WIN)], axis=1
    )
    window = window.transpose(2, 3, 0, 1, 4)
    entry_blocks = (
        random_blocks.reshape(head_count, ctx_count, block_count, RAND)
        .transpose(1, 0, 2, 3)
        .reshape(ctx_count, entry_count)
    )
    owner_of = entry_blocks // block_count
    local_of = entry_blocks % block_count
    entry_ids = jnp.arange(entry_count, dtype=jnp.int32)
    head_of = entry_ids // (block_count * RAND)
    onehot = (owner_of[:, :, None] == jnp.arange(ctx_count, dtype=jnp.int32)[None, None, :]).astype(
        jnp.int32
    )
    before = jnp.cumsum(onehot, axis=1) - onehot
    rank_of = jnp.sum(before * onehot, axis=2)
    slot_hit = (owner_of == own_index)[:, :, None] & (
        rank_of[:, :, None] == jnp.arange(capacity, dtype=jnp.int32)[None, None, :]
    )
    send_index = jnp.sum(
        jnp.where(slot_hit, (local_of * head_count + head_of[None, :])[:, :, None], 0), axis=1
    )
    my_owner = lax.dynamic_index_in_dim(owner_of, own_index, axis=0, keepdims=False)
    my_rank = lax.dynamic_index_in_dim(rank_of, own_index, axis=0, keepdims=False)
    my_place = my_owner * capacity + my_rank
    masked_grad = (
        out_grad.reshape(block_count, BS, features) * keep_rows.astype(jnp.bfloat16)[:, None, None]
    ).reshape(local_rows, features)

    def to_table(tensor):
        return (
            tensor.reshape(block_count, BS, head_count, DH)
            .transpose(0, 2, 1, 3)
            .reshape(block_count * head_count, BS, DH)
        )

    send_keys = picked(to_table(keys), send_index)
    send_values = picked(to_table(values), send_index)
    got_keys, got_values = (
        lax.all_to_all(send_keys, "ctx", split_axis=0, concat_axis=0, tiled=True),
        lax.all_to_all(send_values, "ctx", split_axis=0, concat_axis=0, tiled=True),
    )
    random_keys = picked(got_keys.reshape(ctx_count * capacity, BS, DH), my_place).reshape(
        head_count, block_count, RAND * BS, DH
    )
    random_values = picked(got_values.reshape(ctx_count * capacity, BS, DH), my_place).reshape(
        head_count, block_count, RAND * BS, DH
    )
    query_heads = queries.reshape(block_count, BS, head_count, DH).transpose(2, 0, 1, 3)
    grad_heads = masked_grad.reshape(block_count, BS, head_count, DH).transpose(2, 0, 1, 3)
    global_key_heads = global_key.transpose(1, 0, 2)
    global_value_heads = global_value.transpose(1, 0, 2)
    window_cols = WIN * BS
    random_end = (WIN + RAND) * BS

    def head_work(inputs):
        (
            query_head,
            grad_head,
            win_keys,
            win_values,
            rand_keys,
            rand_values,
            glob_keys,
            glob_values,
        ) = inputs
        key_list = jnp.concatenate(
            [
                win_keys,
                rand_keys,
                jnp.broadcast_to(glob_keys[None], (block_count,) + glob_keys.shape),
            ],
            axis=1,
        )
        value_list = jnp.concatenate(
            [
                win_values,
                rand_values,
                jnp.broadcast_to(glob_values[None], (block_count,) + glob_values.shape),
            ],
            axis=1,
        )
        output, logsum, deltas, probs, dscores, dquery = sparse_rows(
            query_head, key_list, value_list, grad_head, scaling
        )
        win_dk = (
            jnp.einsum(
                "nqk,nqd->nkd",
                dscores[:, :, :window_cols],
                query_head,
                preferred_element_type=jnp.float32,
            )
            * scaling
        )
        win_dv = jnp.einsum(
            "nqk,nqd->nkd", probs[:, :, :window_cols], grad_head, preferred_element_type=jnp.float32
        )
        glob_dk = (
            jnp.einsum(
                "nqk,nqd->kd",
                dscores[:, :, random_end:],
                query_head,
                preferred_element_type=jnp.float32,
            )
            * scaling
        )
        glob_dv = jnp.einsum(
            "nqk,nqd->kd", probs[:, :, random_end:], grad_head, preferred_element_type=jnp.float32
        )
        win_dk = win_dk.reshape(block_count, WIN, BS, DH)
        win_dv = win_dv.reshape(block_count, WIN, BS, DH)
        ext_dk = sum(
            (
                jnp.pad(win_dk[:, shift_by], ((shift_by, WIN - 1 - shift_by), (0, 0), (0, 0)))
                for shift_by in range(WIN)
            )
        )
        ext_dv = sum(
            (
                jnp.pad(win_dv[:, shift_by], ((shift_by, WIN - 1 - shift_by), (0, 0), (0, 0)))
                for shift_by in range(WIN)
            )
        )
        rand_dk = (
            jnp.einsum(
                "nqk,nqd->nkd",
                dscores[:, :, window_cols:random_end],
                query_head,
                preferred_element_type=jnp.float32,
            )
            * scaling
        )
        rand_dv = jnp.einsum(
            "nqk,nqd->nkd",
            probs[:, :, window_cols:random_end],
            grad_head,
            preferred_element_type=jnp.float32,
        )
        return (output, logsum, deltas, dquery, ext_dk, ext_dv, glob_dk, glob_dv, rand_dk, rand_dv)

    results = lax.map(
        head_work,
        (
            query_heads,
            grad_heads,
            window[0],
            window[1],
            random_keys,
            random_values,
            global_key_heads,
            global_value_heads,
        ),
    )
    output_heads, logsums, deltas, dquery_heads, ext_dk, ext_dv, glob_dk, glob_dv = results[:8]
    query_total, glob_dk_total, glob_dv_total = lax.psum((query_part, glob_dk, glob_dv), "ctx")
    rim_low = jnp.stack([ext_dk[:, 0], ext_dv[:, 0]], axis=0)
    rim_high = jnp.stack([ext_dk[:, block_count + 1], ext_dv[:, block_count + 1]], axis=0)
    from_next = from_behind(rim_low.astype(jnp.bfloat16), "ctx", -1).astype(rim_low.dtype)
    from_prev = from_behind(rim_high.astype(jnp.bfloat16), "ctx", 1).astype(rim_high.dtype)
    key_heads = ext_dk[:, 1 : block_count + 1]
    value_heads = ext_dv[:, 1 : block_count + 1]
    key_heads = key_heads.at[:, 0].add(from_prev[0]).at[:, block_count - 1].add(from_next[0])
    value_heads = value_heads.at[:, 0].add(from_prev[1]).at[:, block_count - 1].add(from_next[1])
    rand_dk = results[8].reshape(entry_count, BS, DH)
    rand_dv = results[9].reshape(entry_count, BS, DH)
    out_keys = (
        jnp.zeros((ctx_count * capacity, BS, DH), jnp.float32)
        .at[my_place]
        .set(rand_dk)
        .reshape(ctx_count, capacity, BS, DH)
    )
    out_values = (
        jnp.zeros((ctx_count * capacity, BS, DH), jnp.float32)
        .at[my_place]
        .set(rand_dv)
        .reshape(ctx_count, capacity, BS, DH)
    )
    back_keys, back_values = (
        lax.all_to_all(out_keys, "ctx", split_axis=0, concat_axis=0, tiled=True),
        lax.all_to_all(out_values, "ctx", split_axis=0, concat_axis=0, tiled=True),
    )
    back_keys = back_keys.reshape(ctx_count * capacity, BS, DH)
    back_values = back_values.reshape(ctx_count * capacity, BS, DH)
    flat_index = send_index.reshape(-1)
    table_keys = (
        jnp.zeros((block_count * head_count, BS, DH), jnp.float32).at[flat_index].add(back_keys)
    )
    table_values = (
        jnp.zeros((block_count * head_count, BS, DH), jnp.float32).at[flat_index].add(back_values)
    )
    key_heads = key_heads + table_keys.reshape(block_count, head_count, BS, DH).transpose(
        1, 0, 2, 3
    )
    value_heads = value_heads + table_values.reshape(block_count, head_count, BS, DH).transpose(
        1, 0, 2, 3
    )

    def place_global(tensor):
        return jnp.sum(global_hit[None, :, :, None, None] * tensor[:, None], axis=2)

    key_heads = key_heads + place_global(glob_dk_total.reshape(head_count, GLOBAL, BS, DH))
    value_heads = value_heads + place_global(glob_dv_total.reshape(head_count, GLOBAL, BS, DH))
    key_heads = key_heads + key_from_global.reshape(block_count, BS, head_count, DH).transpose(
        2, 0, 1, 3
    )
    value_heads = value_heads + value_from_global.reshape(
        block_count, BS, head_count, DH
    ).transpose(2, 0, 1, 3)
    query_heads_total = dquery_heads + place_global(
        query_total.reshape(GLOBAL, BS, head_count, DH).transpose(2, 0, 1, 3)
    )
    output_total = output_heads.astype(jnp.float32) * keep_rows[None, :, None, None]
    output_total = output_total + place_global(
        global_out.astype(jnp.float32).reshape(GLOBAL, BS, head_count, DH).transpose(2, 0, 1, 3)
    )

    def to_rows(tensor):
        return tensor.transpose(1, 2, 0, 3).reshape(local_rows, features).astype(jnp.bfloat16)

    return (
        to_rows(output_total),
        to_rows(query_heads_total),
        to_rows(key_heads),
        to_rows(value_heads),
    )


Q, K, V, G = range(4)
LOG2E = 1.4426950408889634
VMEM_LIMIT = 40 * 1024 * 1024
GROUP = 4
TILE_W = 256
TILE_D = 128


def peer(step):
    me = lax.axis_index("ctx")
    return (me // 2 + step // 2) % 2 * 2 + (me % 2 + step % 2) % 2


def heads_kernel(
    random_hbm,
    global_hbm,
    q_ref,
    k_ref,
    v_ref,
    g_ref,
    att_ref,
    dq_ref,
    dk_ref,
    dv_ref,
    inb,
    outb,
    scores_buf,
    weights_buf,
    dscores_buf,
    share,
    att_buf,
    dk_acc,
    dv_acc,
    bias,
    k_t,
    v_t,
    own_in,
    own_out,
    in_send,
    in_recv,
    out_send,
    out_recv,
    relay,
    random_ref,
    global_ref,
    list_sem,
):
    n = GROUP
    me = lax.axis_index("ctx")
    rows = q_ref.shape[0]
    seq = n * rows
    blocks = seq // BS
    scaling = DH ** (-0.5)
    sources = (q_ref, k_ref, v_ref, g_ref)
    targets = (att_ref, dq_ref, dk_ref, dv_ref)

    def at_rows(device):
        return pl.ds(pl.multiple_of(device * rows, rows), rows)

    def at_head(device):
        return pl.ds(pl.multiple_of(device * DH, DH), DH)

    def in_copy(array, step, land):
        other = peer(step)
        return pltpu.make_async_remote_copy(
            src_ref=sources[array].at[:, at_head(other)],
            dst_ref=inb.at[array, at_rows(land)],
            send_sem=in_send.at[array, step - 1],
            recv_sem=in_recv.at[array, step - 1],
            device_id={"ctx": other},
            device_id_type=pl.DeviceIdType.MESH,
        )

    def out_copy(array, step, land):
        other = peer(step)
        return pltpu.make_async_remote_copy(
            src_ref=outb.at[array, at_rows(other)],
            dst_ref=targets[array].at[:, at_head(land)],
            send_sem=out_send.at[array, step - 1],
            recv_sem=out_recv.at[array, step - 1],
            device_id={"ctx": other},
            device_id_type=pl.DeviceIdType.MESH,
        )

    def own_copy_in(array):
        return pltpu.make_async_copy(
            sources[array].at[:, at_head(me)], inb.at[array, at_rows(me)], own_in.at[array]
        )

    def own_copy_out(array):
        return pltpu.make_async_copy(
            outb.at[array, at_rows(me)], targets[array].at[:, at_head(me)], own_out.at[array]
        )

    def arrived(array, step):
        if isinstance(step, int) and step == 0:
            own_copy_in(array).wait()
        else:
            in_copy(array, step, peer(step)).wait_recv()

    def leave(array, step):
        own = isinstance(step, int) and step == 0
        (own_copy_out(array) if own else out_copy(array, step, me)).start()

    core = me % 2
    first, last = 3 - core, 2 + core
    barrier = pltpu.get_barrier_semaphore()

    def greet(semaphore, step):
        pl.semaphore_signal(
            semaphore, inc=1, device_id={"ctx": peer(step)}, device_id_type=pl.DeviceIdType.MESH
        )

    def send_rest():
        for array in (K, V):
            in_copy(array, last, me).start()
        for array in (Q, G):
            in_copy(array, first, me).start()
            in_copy(array, last, me).start()

    greet(barrier, 2)

    @pl.when(core == 1)
    def _():
        greet(barrier, 3)
        pl.semaphore_wait(barrier, 1)
        for array in (K, V):
            in_copy(array, 2, me).start()

    @pl.when(core == 0)
    def _():
        pl.semaphore_wait(barrier, 2)
        greet(relay, 3)
        for array in (K, V):
            in_copy(array, 3, me).start()
        send_rest()
        greet(relay, 2)

    random_copy = pltpu.make_async_copy(random_hbm, random_ref, list_sem.at[0])
    global_copy = pltpu.make_async_copy(global_hbm, global_ref, list_sem.at[1])
    random_copy.start()
    global_copy.start()
    for array in (K, V, Q, G):
        own_copy_in(array).start()
    pl.semaphore_wait(relay, 1)

    @pl.when(core == 1)
    def _():
        send_rest()

    for array in (K, V, Q, G):
        in_copy(array, 1, me).start()

    random_copy.wait()
    global_copy.wait()
    key_block = lax.broadcasted_iota(jnp.int32, (blocks, BS), 0)
    global_a, global_b = (global_ref[0], global_ref[1])
    per_device = rows // BS
    for block in range(blocks):
        query_block = jnp.full((blocks, BS), block, jnp.int32)
        named = [(block - 1) % blocks, block, (block + 1) % blocks]
        named += [random_ref[entry, me, block] for entry in range(RAND)]
        named += [global_a, global_b]
        count = sum((key_block == one).astype(jnp.int32) for one in named)
        is_global = (query_block == global_a) | (query_block == global_b)
        count = jnp.where(is_global, 1, count).astype(jnp.float32)
        level = jnp.where(count > 0.5, jnp.log2(jnp.maximum(count, 1.0)), -1e30)
        lanes = slice(block % per_device * BS, block % per_device * BS + BS)
        bias[block // per_device, :, lanes] = level

    contract_last = (((1,), (1,)), ((), ()))

    def folded(tile, combine):
        return combine(tile.reshape(-1, 8, rows), axis=0)

    def weigh(step):
        arrived(Q, step)
        owner = peer(step)
        query = inb[Q, at_rows(owner)]
        highest = jnp.full((8, rows), -3e38, jnp.float32)
        for start in range(0, seq, TILE_W):
            part = slice(start, start + TILE_W)
            scores = lax.dot_general(
                inb[K, part], query, contract_last, preferred_element_type=jnp.float32
            )
            level = bias[owner, start // BS : (start + TILE_W) // BS]
            scores = (
                scores.reshape(-1, BS, rows) * (scaling * LOG2E) + level[:, None, :]
            ).reshape(TILE_W, rows)
            scores_buf[part] = scores
            highest = jnp.maximum(highest, folded(scores, jnp.max))
        highest = jnp.max(highest, axis=0, keepdims=True)
        total = jnp.zeros((8, rows), jnp.float32)
        for start in range(0, seq, TILE_W):
            part = slice(start, start + TILE_W)
            weights = jnp.exp2(scores_buf[part] - highest)
            total = total + folded(weights, jnp.sum)
            weights_buf[step, part] = weights.astype(jnp.bfloat16)
        share[step] = 1.0 / jnp.sum(total, axis=0, keepdims=True)

    def attend(step):
        att_t = jnp.dot(v_t[...], weights_buf[step], preferred_element_type=jnp.float32)
        att_t = (att_t * share[step]).astype(jnp.bfloat16).astype(jnp.float32)
        outb[0, at_rows(peer(step))] = att_t.T.astype(jnp.bfloat16)
        att_buf[step] = att_t
        leave(0, step)

    def differentiate(step, opening):
        arrived(G, step)
        owner = peer(step)
        query_t = inb[Q, at_rows(owner)].astype(jnp.float32).T
        grad = inb[G, at_rows(owner)]
        grad_t = grad.astype(jnp.float32).T
        delta = jnp.sum(grad_t * att_buf[step], axis=0, keepdims=True)
        for start in range(0, seq, TILE_D):
            part = slice(start, start + TILE_D)
            dprobs = lax.dot_general(
                inb[V, part], grad, contract_last, preferred_element_type=jnp.float32
            )
            weights = weights_buf[step, part].astype(jnp.float32)
            dscores_buf[part] = (weights * (dprobs - delta)).astype(jnp.bfloat16)
        dq_t = jnp.dot(k_t[...], dscores_buf[...], preferred_element_type=jnp.float32)
        dq_t = dq_t * (share[step] * scaling)
        outb[1, at_rows(owner)] = dq_t.T.astype(jnp.bfloat16)
        leave(1, step)
        grad_share = (grad_t * share[step]).astype(jnp.bfloat16)
        query_share = (query_t * share[step]).astype(jnp.bfloat16)
        dv = lax.dot_general(
            weights_buf[step], grad_share, contract_last, preferred_element_type=jnp.float32
        )
        dk = lax.dot_general(
            dscores_buf[...], query_share, contract_last, preferred_element_type=jnp.float32
        )
        dv_acc[...] = dv if opening else dv_acc[...] + dv
        dk_acc[...] = dk if opening else dk_acc[...] + dk

    for step in range(n):
        arrived(K, step)
    k_t[...] = inb[K].T
    weigh(0)
    weigh(1)
    for step in range(n):
        arrived(V, step)
    v_t[...] = inb[V].T
    attend(0)
    differentiate(0, True)
    for step in (first, last):
        weigh(step)
        attend(step)
    differentiate(first, False)
    attend(1)
    differentiate(1, False)
    differentiate(last, False)

    outb[2] = (dk_acc[...] * scaling).astype(jnp.bfloat16)
    outb[3] = dv_acc[...].astype(jnp.bfloat16)
    for step in (2, 3, 1, 0):
        for array in (2, 3):
            leave(array, step)

    for array in range(4):
        own_copy_out(array).wait()
        for step in range(1, n):
            in_copy(array, step, me).wait_send()
            out_copy(array, step, me).wait_send()
            out_copy(array, step, peer(step)).wait_recv()


def place_kernel(*refs):
    copies = [
        pltpu.make_async_copy(refs[array], refs[4 + array], refs[8].at[array])
        for array in range(4)
    ]
    for copy in copies:
        copy.start()
    for copy in copies:
        copy.wait()


def by_heads(queries, keys, values, out_grad, random_blocks, global_blocks):
    n = GROUP
    rows, features = queries.shape
    seq = n * rows
    blocks = seq // BS
    anywhere = pl.BlockSpec(memory_space=pl.ANY)
    results = pl.pallas_call(
        heads_kernel,
        out_shape=[jax.ShapeDtypeStruct((rows, features), jnp.bfloat16)] * 4,
        in_specs=[anywhere] * 6,
        out_specs=[anywhere] * 4,
        scratch_shapes=[
            pltpu.VMEM((4, seq, DH), jnp.bfloat16),
            pltpu.VMEM((4, seq, DH), jnp.bfloat16),
            pltpu.VMEM((seq, rows), jnp.float32),
            pltpu.VMEM((n, seq, rows), jnp.bfloat16),
            pltpu.VMEM((seq, rows), jnp.bfloat16),
            pltpu.VMEM((n, 1, rows), jnp.float32),
            pltpu.VMEM((n, DH, rows), jnp.float32),
            pltpu.VMEM((seq, DH), jnp.float32),
            pltpu.VMEM((seq, DH), jnp.float32),
            pltpu.VMEM((n, blocks, rows), jnp.float32),
            pltpu.VMEM((DH, seq), jnp.bfloat16),
            pltpu.VMEM((DH, seq), jnp.bfloat16),
            pltpu.SemaphoreType.DMA((4,)),
            pltpu.SemaphoreType.DMA((4,)),
            pltpu.SemaphoreType.DMA((4, n - 1)),
            pltpu.SemaphoreType.DMA((4, n - 1)),
            pltpu.SemaphoreType.DMA((4, n - 1)),
            pltpu.SemaphoreType.DMA((4, n - 1)),
            pltpu.SemaphoreType.REGULAR,
            pltpu.SMEM((RAND, n, blocks), jnp.int32),
            pltpu.SMEM((GLOBAL,), jnp.int32),
            pltpu.SemaphoreType.DMA((2,)),
        ],
        compiler_params=pltpu.CompilerParams(
            collective_id=0, has_side_effects=True, vmem_limit_bytes=VMEM_LIMIT
        ),
    )(
        *(
            pltpu.with_memory_space_constraint(array, pltpu.HBM)
            for array in (
                random_blocks.transpose(2, 0, 1),
                global_blocks,
                queries,
                keys,
                values,
                out_grad,
            )
        )
    )
    return pl.pallas_call(
        place_kernel,
        out_shape=[jax.ShapeDtypeStruct((rows, features), jnp.bfloat16)] * 4,
        in_specs=[anywhere] * 4,
        out_specs=[anywhere] * 4,
        scratch_shapes=[pltpu.SemaphoreType.DMA((4,))],
        compiler_params=pltpu.CompilerParams(vmem_limit_bytes=VMEM_LIMIT),
    )(*results)


def solution(mesh):
    in_specs = (
        P(("dp", "ctx"), "head"),
        P(("dp", "ctx"), "head"),
        P(("dp", "ctx"), "head"),
        P(("dp", "ctx"), "head"),
        P(("dp", "head"), None, None),
        P("dp"),
    )
    out_specs = (
        P(("dp", "ctx"), "head"),
        P(("dp", "ctx"), "head"),
        P(("dp", "ctx"), "head"),
        P(("dp", "ctx"), "head"),
    )
    ctx_count = mesh.shape["ctx"]

    def body(queries, *rest):
        heads = queries.shape[1] // DH
        if heads == ctx_count == GROUP:
            return by_heads(queries, *rest)
        return on_device(queries, *rest)

    return jax.shard_map(
        body, mesh=mesh, in_specs=in_specs, out_specs=out_specs, check_vma=False
    )
```

```python
import jax
import jax.numpy as jnp
from jax import lax
from jax.experimental import pallas as pl
from jax.experimental.pallas import tpu as pltpu
from jax.sharding import PartitionSpec as P

DH = 128
BS = 128
WIN = 3
RAND = 3
GLOBAL = 2


def broadcast(value, axis, source):
    kept = jnp.where(lax.axis_index(axis) == source, value, 0).astype(value.dtype)
    return lax.psum(kept, axis)


def merged(part, axis, combine):
    gathered = jax.tree.map(lambda a: lax.all_gather(a, axis), part)

    def take(source):
        return jax.tree.map(lambda a: lax.dynamic_index_in_dim(a, source, 0, False), gathered)

    return lax.fori_loop(
        1, lax.axis_size(axis), lambda source, state: combine(state, take(source)), take(0)
    )


def extended(value, sides, width):
    for axis, dim in sides:
        size, length = (lax.axis_size(axis), value.shape[dim])
        up = [(i, (i + 1) % size) for i in range(size)]
        down = [(j, i) for i, j in up]
        last = lax.slice_in_dim(value, length - width, length, axis=dim)
        first = lax.slice_in_dim(value, 0, width, axis=dim)
        before = lax.ppermute(last, axis, up)
        after = lax.ppermute(first, axis, down)
        value = jnp.concatenate([before, value, after], axis=dim)
    return value


def from_behind(value, axis, by):
    length = lax.axis_size(axis)
    return lax.ppermute(value, axis, [(i, (i + by) % length) for i in range(length)])


def picked(table, index):
    rows = lax.map(
        lambda one: lax.dynamic_index_in_dim(table, one, 0, False), index.reshape(-1)
    )
    return rows.reshape(index.shape + table.shape[1:])


def combine_stats(first_pair, second_pair):
    highest = jnp.maximum(first_pair[0], second_pair[0])
    summed = first_pair[1] * jnp.exp(first_pair[0] - highest) + second_pair[1] * jnp.exp(
        second_pair[0] - highest
    )
    return (highest, summed)


def sparse_rows(query_head, key_list, value_list, grad_head, scaling):
    scores = (
        jnp.einsum("nqd,nkd->nqk", query_head, key_list, preferred_element_type=jnp.float32)
        * scaling
    )
    highest = jnp.max(scores, axis=-1, keepdims=True)
    logsum = highest + jnp.log(jnp.sum(jnp.exp(scores - highest), axis=-1, keepdims=True))
    probs = jnp.exp(scores - logsum).astype(jnp.bfloat16)
    output = jnp.einsum(
        "nqk,nkd->nqd", probs, value_list, preferred_element_type=jnp.float32
    ).astype(jnp.bfloat16)
    deltas = jnp.sum(
        grad_head.astype(jnp.float32) * output.astype(jnp.float32), axis=-1, keepdims=True
    )
    dprobs = jnp.einsum("nqd,nkd->nqk", grad_head, value_list, preferred_element_type=jnp.float32)
    dscores = (probs.astype(jnp.float32) * (dprobs - deltas)).astype(jnp.bfloat16)
    dquery = (
        jnp.einsum("nqk,nkd->nqd", dscores, key_list, preferred_element_type=jnp.float32) * scaling
    )
    return (output, logsum[..., 0], deltas[..., 0], probs, dscores, dquery)


def on_device(queries, keys, values, out_grad, random_blocks, global_blocks):
    ctx_count = lax.axis_size("ctx")
    own_index = lax.axis_index("ctx")
    head_count = random_blocks.shape[0]
    local_rows = queries.shape[0]
    block_count = local_rows // BS
    features = queries.shape[1]
    scaling = DH ** (-0.5)
    entry_count = head_count * block_count * RAND
    capacity = (entry_count + ctx_count - 1) // ctx_count
    block_ids = own_index * block_count + jnp.arange(block_count, dtype=jnp.int32)
    global_hit = (block_ids[:, None] == global_blocks[None, :]).astype(jnp.float32)
    keep_rows = 1.0 - jnp.sum(global_hit, axis=1)
    stacked = jnp.stack([queries, keys, values, out_grad], axis=0)
    received = []
    for position in range(GLOBAL):
        holder_index = global_blocks[position] // block_count
        offset = global_blocks[position] % block_count * BS
        block_piece = lax.dynamic_slice_in_dim(stacked, offset, BS, axis=1)
        received.append(broadcast(block_piece, "ctx", holder_index))
    global_data = jnp.stack(received, axis=1).reshape(4, GLOBAL * BS, head_count, DH)
    global_query = global_data[0]
    global_key = global_data[1]
    global_value = global_data[2]
    global_grad = global_data[3]
    keys_split = keys.reshape(local_rows, head_count, DH)
    values_split = values.reshape(local_rows, head_count, DH)
    global_scores = (
        jnp.einsum("qhd,khd->hqk", global_query, keys_split, preferred_element_type=jnp.float32)
        * scaling
    )
    local_max = jnp.max(global_scores, axis=-1)
    local_sum = jnp.sum(jnp.exp(global_scores - local_max[..., None]), axis=-1)
    merged_max, merged_sum = merged((local_max, local_sum), "ctx", combine_stats)
    global_lse = merged_max + jnp.log(merged_sum)
    global_probs = jnp.exp(global_scores - global_lse[..., None]).astype(jnp.bfloat16)
    partial_out = jnp.einsum(
        "hqk,khd->qhd", global_probs, values_split, preferred_element_type=jnp.float32
    )
    global_out = lax.psum(partial_out, "ctx").astype(jnp.bfloat16)
    global_delta = jnp.sum(
        global_grad.astype(jnp.float32) * global_out.astype(jnp.float32), axis=-1
    ).T
    global_dprobs = jnp.einsum(
        "qhd,khd->hqk", global_grad, values_split, preferred_element_type=jnp.float32
    )
    global_dscores = (
        global_probs.astype(jnp.float32) * (global_dprobs - global_delta[..., None])
    ).astype(jnp.bfloat16)
    query_part = (
        jnp.einsum("hqk,khd->qhd", global_dscores, keys_split, preferred_element_type=jnp.float32)
        * scaling
    )
    key_from_global = (
        jnp.einsum("hqk,qhd->khd", global_dscores, global_query, preferred_element_type=jnp.float32)
        * scaling
    )
    value_from_global = jnp.einsum(
        "hqk,qhd->khd", global_probs, global_grad, preferred_element_type=jnp.float32
    )
    paired = jnp.stack([keys, values], axis=1)
    padded = extended(paired, (("ctx", 0),), BS)
    padded = padded.reshape(block_count + 2, BS, 2, head_count, DH)
    window = jnp.concatenate(
        [padded[start_block : start_block + block_count] for start_block in range(WIN)], axis=1
    )
    window = window.transpose(2, 3, 0, 1, 4)
    entry_blocks = (
        random_blocks.reshape(head_count, ctx_count, block_count, RAND)
        .transpose(1, 0, 2, 3)
        .reshape(ctx_count, entry_count)
    )
    owner_of = entry_blocks // block_count
    local_of = entry_blocks % block_count
    entry_ids = jnp.arange(entry_count, dtype=jnp.int32)
    head_of = entry_ids // (block_count * RAND)
    onehot = (owner_of[:, :, None] == jnp.arange(ctx_count, dtype=jnp.int32)[None, None, :]).astype(
        jnp.int32
    )
    before = jnp.cumsum(onehot, axis=1) - onehot
    rank_of = jnp.sum(before * onehot, axis=2)
    slot_hit = (owner_of == own_index)[:, :, None] & (
        rank_of[:, :, None] == jnp.arange(capacity, dtype=jnp.int32)[None, None, :]
    )
    send_index = jnp.sum(
        jnp.where(slot_hit, (local_of * head_count + head_of[None, :])[:, :, None], 0), axis=1
    )
    my_owner = lax.dynamic_index_in_dim(owner_of, own_index, axis=0, keepdims=False)
    my_rank = lax.dynamic_index_in_dim(rank_of, own_index, axis=0, keepdims=False)
    my_place = my_owner * capacity + my_rank
    masked_grad = (
        out_grad.reshape(block_count, BS, features) * keep_rows.astype(jnp.bfloat16)[:, None, None]
    ).reshape(local_rows, features)

    def to_table(tensor):
        return (
            tensor.reshape(block_count, BS, head_count, DH)
            .transpose(0, 2, 1, 3)
            .reshape(block_count * head_count, BS, DH)
        )

    send_keys = picked(to_table(keys), send_index)
    send_values = picked(to_table(values), send_index)
    got_keys, got_values = (
        lax.all_to_all(send_keys, "ctx", split_axis=0, concat_axis=0, tiled=True),
        lax.all_to_all(send_values, "ctx", split_axis=0, concat_axis=0, tiled=True),
    )
    random_keys = picked(got_keys.reshape(ctx_count * capacity, BS, DH), my_place).reshape(
        head_count, block_count, RAND * BS, DH
    )
    random_values = picked(got_values.reshape(ctx_count * capacity, BS, DH), my_place).reshape(
        head_count, block_count, RAND * BS, DH
    )
    query_heads = queries.reshape(block_count, BS, head_count, DH).transpose(2, 0, 1, 3)
    grad_heads = masked_grad.reshape(block_count, BS, head_count, DH).transpose(2, 0, 1, 3)
    global_key_heads = global_key.transpose(1, 0, 2)
    global_value_heads = global_value.transpose(1, 0, 2)
    window_cols = WIN * BS
    random_end = (WIN + RAND) * BS

    def head_work(inputs):
        (
            query_head,
            grad_head,
            win_keys,
            win_values,
            rand_keys,
            rand_values,
            glob_keys,
            glob_values,
        ) = inputs
        key_list = jnp.concatenate(
            [
                win_keys,
                rand_keys,
                jnp.broadcast_to(glob_keys[None], (block_count,) + glob_keys.shape),
            ],
            axis=1,
        )
        value_list = jnp.concatenate(
            [
                win_values,
                rand_values,
                jnp.broadcast_to(glob_values[None], (block_count,) + glob_values.shape),
            ],
            axis=1,
        )
        output, logsum, deltas, probs, dscores, dquery = sparse_rows(
            query_head, key_list, value_list, grad_head, scaling
        )
        win_dk = (
            jnp.einsum(
                "nqk,nqd->nkd",
                dscores[:, :, :window_cols],
                query_head,
                preferred_element_type=jnp.float32,
            )
            * scaling
        )
        win_dv = jnp.einsum(
            "nqk,nqd->nkd", probs[:, :, :window_cols], grad_head, preferred_element_type=jnp.float32
        )
        glob_dk = (
            jnp.einsum(
                "nqk,nqd->kd",
                dscores[:, :, random_end:],
                query_head,
                preferred_element_type=jnp.float32,
            )
            * scaling
        )
        glob_dv = jnp.einsum(
            "nqk,nqd->kd", probs[:, :, random_end:], grad_head, preferred_element_type=jnp.float32
        )
        win_dk = win_dk.reshape(block_count, WIN, BS, DH)
        win_dv = win_dv.reshape(block_count, WIN, BS, DH)
        ext_dk = sum(
            (
                jnp.pad(win_dk[:, shift_by], ((shift_by, WIN - 1 - shift_by), (0, 0), (0, 0)))
                for shift_by in range(WIN)
            )
        )
        ext_dv = sum(
            (
                jnp.pad(win_dv[:, shift_by], ((shift_by, WIN - 1 - shift_by), (0, 0), (0, 0)))
                for shift_by in range(WIN)
            )
        )
        rand_dk = (
            jnp.einsum(
                "nqk,nqd->nkd",
                dscores[:, :, window_cols:random_end],
                query_head,
                preferred_element_type=jnp.float32,
            )
            * scaling
        )
        rand_dv = jnp.einsum(
            "nqk,nqd->nkd",
            probs[:, :, window_cols:random_end],
            grad_head,
            preferred_element_type=jnp.float32,
        )
        return (output, logsum, deltas, dquery, ext_dk, ext_dv, glob_dk, glob_dv, rand_dk, rand_dv)

    results = lax.map(
        head_work,
        (
            query_heads,
            grad_heads,
            window[0],
            window[1],
            random_keys,
            random_values,
            global_key_heads,
            global_value_heads,
        ),
    )
    output_heads, logsums, deltas, dquery_heads, ext_dk, ext_dv, glob_dk, glob_dv = results[:8]
    query_total, glob_dk_total, glob_dv_total = lax.psum((query_part, glob_dk, glob_dv), "ctx")
    rim_low = jnp.stack([ext_dk[:, 0], ext_dv[:, 0]], axis=0)
    rim_high = jnp.stack([ext_dk[:, block_count + 1], ext_dv[:, block_count + 1]], axis=0)
    from_next = from_behind(rim_low.astype(jnp.bfloat16), "ctx", -1).astype(rim_low.dtype)
    from_prev = from_behind(rim_high.astype(jnp.bfloat16), "ctx", 1).astype(rim_high.dtype)
    key_heads = ext_dk[:, 1 : block_count + 1]
    value_heads = ext_dv[:, 1 : block_count + 1]
    key_heads = key_heads.at[:, 0].add(from_prev[0]).at[:, block_count - 1].add(from_next[0])
    value_heads = value_heads.at[:, 0].add(from_prev[1]).at[:, block_count - 1].add(from_next[1])
    rand_dk = results[8].reshape(entry_count, BS, DH)
    rand_dv = results[9].reshape(entry_count, BS, DH)
    out_keys = (
        jnp.zeros((ctx_count * capacity, BS, DH), jnp.float32)
        .at[my_place]
        .set(rand_dk)
        .reshape(ctx_count, capacity, BS, DH)
    )
    out_values = (
        jnp.zeros((ctx_count * capacity, BS, DH), jnp.float32)
        .at[my_place]
        .set(rand_dv)
        .reshape(ctx_count, capacity, BS, DH)
    )
    back_keys, back_values = (
        lax.all_to_all(out_keys, "ctx", split_axis=0, concat_axis=0, tiled=True),
        lax.all_to_all(out_values, "ctx", split_axis=0, concat_axis=0, tiled=True),
    )
    back_keys = back_keys.reshape(ctx_count * capacity, BS, DH)
    back_values = back_values.reshape(ctx_count * capacity, BS, DH)
    flat_index = send_index.reshape(-1)
    table_keys = (
        jnp.zeros((block_count * head_count, BS, DH), jnp.float32).at[flat_index].add(back_keys)
    )
    table_values = (
        jnp.zeros((block_count * head_count, BS, DH), jnp.float32).at[flat_index].add(back_values)
    )
    key_heads = key_heads + table_keys.reshape(block_count, head_count, BS, DH).transpose(
        1, 0, 2, 3
    )
    value_heads = value_heads + table_values.reshape(block_count, head_count, BS, DH).transpose(
        1, 0, 2, 3
    )

    def place_global(tensor):
        return jnp.sum(global_hit[None, :, :, None, None] * tensor[:, None], axis=2)

    key_heads = key_heads + place_global(glob_dk_total.reshape(head_count, GLOBAL, BS, DH))
    value_heads = value_heads + place_global(glob_dv_total.reshape(head_count, GLOBAL, BS, DH))
    key_heads = key_heads + key_from_global.reshape(block_count, BS, head_count, DH).transpose(
        2, 0, 1, 3
    )
    value_heads = value_heads + value_from_global.reshape(
        block_count, BS, head_count, DH
    ).transpose(2, 0, 1, 3)
    query_heads_total = dquery_heads + place_global(
        query_total.reshape(GLOBAL, BS, head_count, DH).transpose(2, 0, 1, 3)
    )
    output_total = output_heads.astype(jnp.float32) * keep_rows[None, :, None, None]
    output_total = output_total + place_global(
        global_out.astype(jnp.float32).reshape(GLOBAL, BS, head_count, DH).transpose(2, 0, 1, 3)
    )

    def to_rows(tensor):
        return tensor.transpose(1, 2, 0, 3).reshape(local_rows, features).astype(jnp.bfloat16)

    return (
        to_rows(output_total),
        to_rows(query_heads_total),
        to_rows(key_heads),
        to_rows(value_heads),
    )


Q, K, V, G = range(4)
LOG2E = 1.4426950408889634
VMEM_LIMIT = 40 * 1024 * 1024
GROUP = 4
TILE_W = 256
TILE_D = 128


def peer(step):
    me = lax.axis_index("ctx")
    return (me // 2 + step // 2) % 2 * 2 + (me % 2 + step % 2) % 2


def heads_kernel(
    random_hbm,
    global_hbm,
    q_ref,
    k_ref,
    v_ref,
    g_ref,
    out_ref,
    inb,
    outb,
    scores_buf,
    weights_buf,
    dscores_buf,
    share,
    att_buf,
    dk_acc,
    dv_acc,
    bias,
    k_t,
    v_t,
    own_in,
    own_out,
    in_send,
    in_recv,
    out_send,
    out_recv,
    relay,
    random_ref,
    global_ref,
    list_sem,
):
    n = GROUP
    me = lax.axis_index("ctx")
    rows = q_ref.shape[0]
    seq = n * rows
    blocks = seq // BS
    scaling = DH ** (-0.5)
    sources = (q_ref, k_ref, v_ref, g_ref)

    def at_rows(device):
        return pl.ds(pl.multiple_of(device * rows, rows), rows)

    def at_head(device):
        return pl.ds(pl.multiple_of(device * DH, DH), DH)

    def in_copy(array, step, land):
        other = peer(step)
        return pltpu.make_async_remote_copy(
            src_ref=sources[array].at[:, at_head(other)],
            dst_ref=inb.at[array, at_rows(land)],
            send_sem=in_send.at[array, step - 1],
            recv_sem=in_recv.at[array, step - 1],
            device_id={"ctx": other},
            device_id_type=pl.DeviceIdType.MESH,
        )

    def kind(array):
        return pl.ds(2, 2) if array == 2 else array

    def out_copy(array, step, land):
        other = peer(step)
        return pltpu.make_async_remote_copy(
            src_ref=outb.at[kind(array), at_rows(other)],
            dst_ref=out_ref.at[kind(array), :, at_head(land)],
            send_sem=out_send.at[array, step - 1],
            recv_sem=out_recv.at[array, step - 1],
            device_id={"ctx": other},
            device_id_type=pl.DeviceIdType.MESH,
        )

    def own_copy_in(array):
        return pltpu.make_async_copy(
            sources[array].at[:, at_head(me)], inb.at[array, at_rows(me)], own_in.at[array]
        )

    def own_copy_out(array):
        return pltpu.make_async_copy(
            outb.at[kind(array), at_rows(me)],
            out_ref.at[kind(array), :, at_head(me)],
            own_out.at[array],
        )

    def arrived(array, step):
        if isinstance(step, int) and step == 0:
            own_copy_in(array).wait()
        else:
            in_copy(array, step, peer(step)).wait_recv()

    def leave(array, step):
        own = isinstance(step, int) and step == 0
        (own_copy_out(array) if own else out_copy(array, step, me)).start()

    core = me % 2
    first, last = 3 - core, 2 + core
    barrier = pltpu.get_barrier_semaphore()

    def greet(semaphore, step):
        pl.semaphore_signal(
            semaphore, inc=1, device_id={"ctx": peer(step)}, device_id_type=pl.DeviceIdType.MESH
        )

    def send_rest():
        for array in (K, V):
            in_copy(array, last, me).start()
        for array in (Q, G):
            in_copy(array, first, me).start()
            in_copy(array, last, me).start()

    greet(barrier, 2)

    @pl.when(core == 1)
    def _():
        greet(barrier, 3)
        pl.semaphore_wait(barrier, 1)
        for array in (K, V):
            in_copy(array, 2, me).start()

    @pl.when(core == 0)
    def _():
        pl.semaphore_wait(barrier, 2)
        greet(relay, 3)
        for array in (K, V):
            in_copy(array, 3, me).start()
        send_rest()
        greet(relay, 2)

    random_copy = pltpu.make_async_copy(random_hbm, random_ref, list_sem.at[0])
    global_copy = pltpu.make_async_copy(global_hbm, global_ref, list_sem.at[1])
    random_copy.start()
    global_copy.start()
    for array in (K, V, Q, G):
        own_copy_in(array).start()
    pl.semaphore_wait(relay, 1)

    @pl.when(core == 1)
    def _():
        send_rest()

    for array in (K, V, Q, G):
        in_copy(array, 1, me).start()

    random_copy.wait()
    global_copy.wait()
    key_block = lax.broadcasted_iota(jnp.int32, (blocks, BS), 0)
    global_a, global_b = (global_ref[0], global_ref[1])
    per_device = rows // BS
    for block in range(blocks):
        query_block = jnp.full((blocks, BS), block, jnp.int32)
        named = [(block - 1) % blocks, block, (block + 1) % blocks]
        named += [random_ref[entry, me, block] for entry in range(RAND)]
        named += [global_a, global_b]
        count = sum((key_block == one).astype(jnp.int32) for one in named)
        is_global = (query_block == global_a) | (query_block == global_b)
        count = jnp.where(is_global, 1, count).astype(jnp.float32)
        level = jnp.where(count > 0.5, jnp.log2(jnp.maximum(count, 1.0)), -1e30)
        lanes = slice(block % per_device * BS, block % per_device * BS + BS)
        bias[block // per_device, :, lanes] = level

    contract_last = (((1,), (1,)), ((), ()))

    def folded(tile, combine):
        return combine(tile.reshape(-1, 8, rows), axis=0)

    def weigh(step):
        arrived(Q, step)
        owner = peer(step)
        query = inb[Q, at_rows(owner)]
        highest = jnp.full((8, rows), -3e38, jnp.float32)
        for start in range(0, seq, TILE_W):
            part = slice(start, start + TILE_W)
            scores = lax.dot_general(
                inb[K, part], query, contract_last, preferred_element_type=jnp.float32
            )
            level = bias[owner, start // BS : (start + TILE_W) // BS]
            scores = (
                scores.reshape(-1, BS, rows) * (scaling * LOG2E) + level[:, None, :]
            ).reshape(TILE_W, rows)
            scores_buf[part] = scores
            highest = jnp.maximum(highest, folded(scores, jnp.max))
        highest = jnp.max(highest, axis=0, keepdims=True)
        total = jnp.zeros((8, rows), jnp.float32)
        for start in range(0, seq, TILE_W):
            part = slice(start, start + TILE_W)
            weights = jnp.exp2(scores_buf[part] - highest)
            total = total + folded(weights, jnp.sum)
            weights_buf[step, part] = weights.astype(jnp.bfloat16)
        share[step] = 1.0 / jnp.sum(total, axis=0, keepdims=True)

    def attend(step):
        att_t = jnp.dot(v_t[...], weights_buf[step], preferred_element_type=jnp.float32)
        att_t = (att_t * share[step]).astype(jnp.bfloat16).astype(jnp.float32)
        outb[0, at_rows(peer(step))] = att_t.T.astype(jnp.bfloat16)
        att_buf[step] = att_t
        leave(0, step)

    def differentiate(step, opening):
        arrived(G, step)
        owner = peer(step)
        query_t = inb[Q, at_rows(owner)].astype(jnp.float32).T
        grad = inb[G, at_rows(owner)]
        grad_t = grad.astype(jnp.float32).T
        delta = jnp.sum(grad_t * att_buf[step], axis=0, keepdims=True)
        for start in range(0, seq, TILE_D):
            part = slice(start, start + TILE_D)
            dprobs = lax.dot_general(
                inb[V, part], grad, contract_last, preferred_element_type=jnp.float32
            )
            weights = weights_buf[step, part].astype(jnp.float32)
            dscores_buf[part] = (weights * (dprobs - delta)).astype(jnp.bfloat16)
        dq_t = jnp.dot(k_t[...], dscores_buf[...], preferred_element_type=jnp.float32)
        dq_t = dq_t * (share[step] * scaling)
        outb[1, at_rows(owner)] = dq_t.T.astype(jnp.bfloat16)
        leave(1, step)
        grad_share = (grad_t * share[step]).astype(jnp.bfloat16)
        query_share = (query_t * share[step]).astype(jnp.bfloat16)
        dv = lax.dot_general(
            weights_buf[step], grad_share, contract_last, preferred_element_type=jnp.float32
        )
        dk = lax.dot_general(
            dscores_buf[...], query_share, contract_last, preferred_element_type=jnp.float32
        )
        dv_acc[...] = dv if opening else dv_acc[...] + dv
        dk_acc[...] = dk if opening else dk_acc[...] + dk

    for step in range(n):
        arrived(K, step)
    k_t[...] = inb[K].T
    weigh(0)
    weigh(1)
    for step in range(n):
        arrived(V, step)
    v_t[...] = inb[V].T
    attend(0)
    differentiate(0, True)
    for step in (first, last):
        weigh(step)
        attend(step)
    differentiate(first, False)
    attend(1)
    differentiate(1, False)
    differentiate(last, False)

    outb[2] = (dk_acc[...] * scaling).astype(jnp.bfloat16)
    outb[3] = dv_acc[...].astype(jnp.bfloat16)
    for step in (2, 3, 1, 0):
        leave(2, step)

    for array in range(4):
        for step in range(1, n):
            in_copy(array, step, me).wait_send()
    for array in range(3):
        own_copy_out(array).wait()
        for step in range(1, n):
            out_copy(array, step, me).wait_send()
            out_copy(array, step, peer(step)).wait_recv()


def place_kernel(joint_ref, *refs):
    copies = [
        pltpu.make_async_copy(joint_ref.at[array], refs[array], refs[4].at[array])
        for array in range(4)
    ]
    for copy in copies:
        copy.start()
    for copy in copies:
        copy.wait()


def by_heads(queries, keys, values, out_grad, random_blocks, global_blocks):
    n = GROUP
    rows, features = queries.shape
    seq = n * rows
    blocks = seq // BS
    anywhere = pl.BlockSpec(memory_space=pl.ANY)
    result = pl.pallas_call(
        heads_kernel,
        out_shape=jax.ShapeDtypeStruct((4, rows, features), jnp.bfloat16),
        in_specs=[anywhere] * 6,
        out_specs=anywhere,
        scratch_shapes=[
            pltpu.VMEM((4, seq, DH), jnp.bfloat16),
            pltpu.VMEM((4, seq, DH), jnp.bfloat16),
            pltpu.VMEM((seq, rows), jnp.float32),
            pltpu.VMEM((n, seq, rows), jnp.bfloat16),
            pltpu.VMEM((seq, rows), jnp.bfloat16),
            pltpu.VMEM((n, 1, rows), jnp.float32),
            pltpu.VMEM((n, DH, rows), jnp.float32),
            pltpu.VMEM((seq, DH), jnp.float32),
            pltpu.VMEM((seq, DH), jnp.float32),
            pltpu.VMEM((n, blocks, rows), jnp.float32),
            pltpu.VMEM((DH, seq), jnp.bfloat16),
            pltpu.VMEM((DH, seq), jnp.bfloat16),
            pltpu.SemaphoreType.DMA((4,)),
            pltpu.SemaphoreType.DMA((4,)),
            pltpu.SemaphoreType.DMA((4, n - 1)),
            pltpu.SemaphoreType.DMA((4, n - 1)),
            pltpu.SemaphoreType.DMA((4, n - 1)),
            pltpu.SemaphoreType.DMA((4, n - 1)),
            pltpu.SemaphoreType.REGULAR,
            pltpu.SMEM((RAND, n, blocks), jnp.int32),
            pltpu.SMEM((GLOBAL,), jnp.int32),
            pltpu.SemaphoreType.DMA((2,)),
        ],
        compiler_params=pltpu.CompilerParams(
            collective_id=0, has_side_effects=True, vmem_limit_bytes=VMEM_LIMIT
        ),
    )(
        *(
            pltpu.with_memory_space_constraint(array, pltpu.HBM)
            for array in (
                random_blocks.transpose(2, 0, 1),
                global_blocks,
                queries,
                keys,
                values,
                out_grad,
            )
        )
    )
    return pl.pallas_call(
        place_kernel,
        out_shape=[jax.ShapeDtypeStruct((rows, features), jnp.bfloat16)] * 4,
        in_specs=[anywhere],
        out_specs=[anywhere] * 4,
        scratch_shapes=[pltpu.SemaphoreType.DMA((4,))],
        compiler_params=pltpu.CompilerParams(vmem_limit_bytes=VMEM_LIMIT),
    )(result)


def solution(mesh):
    in_specs = (
        P(("dp", "ctx"), "head"),
        P(("dp", "ctx"), "head"),
        P(("dp", "ctx"), "head"),
        P(("dp", "ctx"), "head"),
        P(("dp", "head"), None, None),
        P("dp"),
    )
    out_specs = (
        P(("dp", "ctx"), "head"),
        P(("dp", "ctx"), "head"),
        P(("dp", "ctx"), "head"),
        P(("dp", "ctx"), "head"),
    )
    ctx_count = mesh.shape["ctx"]

    def body(queries, *rest):
        heads = queries.shape[1] // DH
        if heads == ctx_count == GROUP:
            return by_heads(queries, *rest)
        return on_device(queries, *rest)

    return jax.shard_map(
        body, mesh=mesh, in_specs=in_specs, out_specs=out_specs, check_vma=False
    )
```

```python
import jax
import jax.numpy as jnp
from jax import lax
from jax.experimental import pallas as pl
from jax.experimental.pallas import tpu as pltpu
from jax.sharding import PartitionSpec as P

DH = 128
BS = 128
WIN = 3
RAND = 3
GLOBAL = 2


def broadcast(value, axis, source):
    kept = jnp.where(lax.axis_index(axis) == source, value, 0).astype(value.dtype)
    return lax.psum(kept, axis)


def merged(part, axis, combine):
    gathered = jax.tree.map(lambda a: lax.all_gather(a, axis), part)

    def take(source):
        return jax.tree.map(lambda a: lax.dynamic_index_in_dim(a, source, 0, False), gathered)

    return lax.fori_loop(
        1, lax.axis_size(axis), lambda source, state: combine(state, take(source)), take(0)
    )


def extended(value, sides, width):
    for axis, dim in sides:
        size, length = (lax.axis_size(axis), value.shape[dim])
        up = [(i, (i + 1) % size) for i in range(size)]
        down = [(j, i) for i, j in up]
        last = lax.slice_in_dim(value, length - width, length, axis=dim)
        first = lax.slice_in_dim(value, 0, width, axis=dim)
        before = lax.ppermute(last, axis, up)
        after = lax.ppermute(first, axis, down)
        value = jnp.concatenate([before, value, after], axis=dim)
    return value


def from_behind(value, axis, by):
    length = lax.axis_size(axis)
    return lax.ppermute(value, axis, [(i, (i + by) % length) for i in range(length)])


def picked(table, index):
    rows = lax.map(
        lambda one: lax.dynamic_index_in_dim(table, one, 0, False), index.reshape(-1)
    )
    return rows.reshape(index.shape + table.shape[1:])


def combine_stats(first_pair, second_pair):
    highest = jnp.maximum(first_pair[0], second_pair[0])
    summed = first_pair[1] * jnp.exp(first_pair[0] - highest) + second_pair[1] * jnp.exp(
        second_pair[0] - highest
    )
    return (highest, summed)


def sparse_rows(query_head, key_list, value_list, grad_head, scaling):
    scores = (
        jnp.einsum("nqd,nkd->nqk", query_head, key_list, preferred_element_type=jnp.float32)
        * scaling
    )
    highest = jnp.max(scores, axis=-1, keepdims=True)
    logsum = highest + jnp.log(jnp.sum(jnp.exp(scores - highest), axis=-1, keepdims=True))
    probs = jnp.exp(scores - logsum).astype(jnp.bfloat16)
    output = jnp.einsum(
        "nqk,nkd->nqd", probs, value_list, preferred_element_type=jnp.float32
    ).astype(jnp.bfloat16)
    deltas = jnp.sum(
        grad_head.astype(jnp.float32) * output.astype(jnp.float32), axis=-1, keepdims=True
    )
    dprobs = jnp.einsum("nqd,nkd->nqk", grad_head, value_list, preferred_element_type=jnp.float32)
    dscores = (probs.astype(jnp.float32) * (dprobs - deltas)).astype(jnp.bfloat16)
    dquery = (
        jnp.einsum("nqk,nkd->nqd", dscores, key_list, preferred_element_type=jnp.float32) * scaling
    )
    return (output, logsum[..., 0], deltas[..., 0], probs, dscores, dquery)


def on_device(queries, keys, values, out_grad, random_blocks, global_blocks):
    ctx_count = lax.axis_size("ctx")
    own_index = lax.axis_index("ctx")
    head_count = random_blocks.shape[0]
    local_rows = queries.shape[0]
    block_count = local_rows // BS
    features = queries.shape[1]
    scaling = DH ** (-0.5)
    entry_count = head_count * block_count * RAND
    capacity = (entry_count + ctx_count - 1) // ctx_count
    block_ids = own_index * block_count + jnp.arange(block_count, dtype=jnp.int32)
    global_hit = (block_ids[:, None] == global_blocks[None, :]).astype(jnp.float32)
    keep_rows = 1.0 - jnp.sum(global_hit, axis=1)
    stacked = jnp.stack([queries, keys, values, out_grad], axis=0)
    received = []
    for position in range(GLOBAL):
        holder_index = global_blocks[position] // block_count
        offset = global_blocks[position] % block_count * BS
        block_piece = lax.dynamic_slice_in_dim(stacked, offset, BS, axis=1)
        received.append(broadcast(block_piece, "ctx", holder_index))
    global_data = jnp.stack(received, axis=1).reshape(4, GLOBAL * BS, head_count, DH)
    global_query = global_data[0]
    global_key = global_data[1]
    global_value = global_data[2]
    global_grad = global_data[3]
    keys_split = keys.reshape(local_rows, head_count, DH)
    values_split = values.reshape(local_rows, head_count, DH)
    global_scores = (
        jnp.einsum("qhd,khd->hqk", global_query, keys_split, preferred_element_type=jnp.float32)
        * scaling
    )
    local_max = jnp.max(global_scores, axis=-1)
    local_sum = jnp.sum(jnp.exp(global_scores - local_max[..., None]), axis=-1)
    merged_max, merged_sum = merged((local_max, local_sum), "ctx", combine_stats)
    global_lse = merged_max + jnp.log(merged_sum)
    global_probs = jnp.exp(global_scores - global_lse[..., None]).astype(jnp.bfloat16)
    partial_out = jnp.einsum(
        "hqk,khd->qhd", global_probs, values_split, preferred_element_type=jnp.float32
    )
    global_out = lax.psum(partial_out, "ctx").astype(jnp.bfloat16)
    global_delta = jnp.sum(
        global_grad.astype(jnp.float32) * global_out.astype(jnp.float32), axis=-1
    ).T
    global_dprobs = jnp.einsum(
        "qhd,khd->hqk", global_grad, values_split, preferred_element_type=jnp.float32
    )
    global_dscores = (
        global_probs.astype(jnp.float32) * (global_dprobs - global_delta[..., None])
    ).astype(jnp.bfloat16)
    query_part = (
        jnp.einsum("hqk,khd->qhd", global_dscores, keys_split, preferred_element_type=jnp.float32)
        * scaling
    )
    key_from_global = (
        jnp.einsum("hqk,qhd->khd", global_dscores, global_query, preferred_element_type=jnp.float32)
        * scaling
    )
    value_from_global = jnp.einsum(
        "hqk,qhd->khd", global_probs, global_grad, preferred_element_type=jnp.float32
    )
    paired = jnp.stack([keys, values], axis=1)
    padded = extended(paired, (("ctx", 0),), BS)
    padded = padded.reshape(block_count + 2, BS, 2, head_count, DH)
    window = jnp.concatenate(
        [padded[start_block : start_block + block_count] for start_block in range(WIN)], axis=1
    )
    window = window.transpose(2, 3, 0, 1, 4)
    entry_blocks = (
        random_blocks.reshape(head_count, ctx_count, block_count, RAND)
        .transpose(1, 0, 2, 3)
        .reshape(ctx_count, entry_count)
    )
    owner_of = entry_blocks // block_count
    local_of = entry_blocks % block_count
    entry_ids = jnp.arange(entry_count, dtype=jnp.int32)
    head_of = entry_ids // (block_count * RAND)
    onehot = (owner_of[:, :, None] == jnp.arange(ctx_count, dtype=jnp.int32)[None, None, :]).astype(
        jnp.int32
    )
    before = jnp.cumsum(onehot, axis=1) - onehot
    rank_of = jnp.sum(before * onehot, axis=2)
    slot_hit = (owner_of == own_index)[:, :, None] & (
        rank_of[:, :, None] == jnp.arange(capacity, dtype=jnp.int32)[None, None, :]
    )
    send_index = jnp.sum(
        jnp.where(slot_hit, (local_of * head_count + head_of[None, :])[:, :, None], 0), axis=1
    )
    my_owner = lax.dynamic_index_in_dim(owner_of, own_index, axis=0, keepdims=False)
    my_rank = lax.dynamic_index_in_dim(rank_of, own_index, axis=0, keepdims=False)
    my_place = my_owner * capacity + my_rank
    masked_grad = (
        out_grad.reshape(block_count, BS, features) * keep_rows.astype(jnp.bfloat16)[:, None, None]
    ).reshape(local_rows, features)

    def to_table(tensor):
        return (
            tensor.reshape(block_count, BS, head_count, DH)
            .transpose(0, 2, 1, 3)
            .reshape(block_count * head_count, BS, DH)
        )

    send_keys = picked(to_table(keys), send_index)
    send_values = picked(to_table(values), send_index)
    got_keys, got_values = (
        lax.all_to_all(send_keys, "ctx", split_axis=0, concat_axis=0, tiled=True),
        lax.all_to_all(send_values, "ctx", split_axis=0, concat_axis=0, tiled=True),
    )
    random_keys = picked(got_keys.reshape(ctx_count * capacity, BS, DH), my_place).reshape(
        head_count, block_count, RAND * BS, DH
    )
    random_values = picked(got_values.reshape(ctx_count * capacity, BS, DH), my_place).reshape(
        head_count, block_count, RAND * BS, DH
    )
    query_heads = queries.reshape(block_count, BS, head_count, DH).transpose(2, 0, 1, 3)
    grad_heads = masked_grad.reshape(block_count, BS, head_count, DH).transpose(2, 0, 1, 3)
    global_key_heads = global_key.transpose(1, 0, 2)
    global_value_heads = global_value.transpose(1, 0, 2)
    window_cols = WIN * BS
    random_end = (WIN + RAND) * BS

    def head_work(inputs):
        (
            query_head,
            grad_head,
            win_keys,
            win_values,
            rand_keys,
            rand_values,
            glob_keys,
            glob_values,
        ) = inputs
        key_list = jnp.concatenate(
            [
                win_keys,
                rand_keys,
                jnp.broadcast_to(glob_keys[None], (block_count,) + glob_keys.shape),
            ],
            axis=1,
        )
        value_list = jnp.concatenate(
            [
                win_values,
                rand_values,
                jnp.broadcast_to(glob_values[None], (block_count,) + glob_values.shape),
            ],
            axis=1,
        )
        output, logsum, deltas, probs, dscores, dquery = sparse_rows(
            query_head, key_list, value_list, grad_head, scaling
        )
        win_dk = (
            jnp.einsum(
                "nqk,nqd->nkd",
                dscores[:, :, :window_cols],
                query_head,
                preferred_element_type=jnp.float32,
            )
            * scaling
        )
        win_dv = jnp.einsum(
            "nqk,nqd->nkd", probs[:, :, :window_cols], grad_head, preferred_element_type=jnp.float32
        )
        glob_dk = (
            jnp.einsum(
                "nqk,nqd->kd",
                dscores[:, :, random_end:],
                query_head,
                preferred_element_type=jnp.float32,
            )
            * scaling
        )
        glob_dv = jnp.einsum(
            "nqk,nqd->kd", probs[:, :, random_end:], grad_head, preferred_element_type=jnp.float32
        )
        win_dk = win_dk.reshape(block_count, WIN, BS, DH)
        win_dv = win_dv.reshape(block_count, WIN, BS, DH)
        ext_dk = sum(
            (
                jnp.pad(win_dk[:, shift_by], ((shift_by, WIN - 1 - shift_by), (0, 0), (0, 0)))
                for shift_by in range(WIN)
            )
        )
        ext_dv = sum(
            (
                jnp.pad(win_dv[:, shift_by], ((shift_by, WIN - 1 - shift_by), (0, 0), (0, 0)))
                for shift_by in range(WIN)
            )
        )
        rand_dk = (
            jnp.einsum(
                "nqk,nqd->nkd",
                dscores[:, :, window_cols:random_end],
                query_head,
                preferred_element_type=jnp.float32,
            )
            * scaling
        )
        rand_dv = jnp.einsum(
            "nqk,nqd->nkd",
            probs[:, :, window_cols:random_end],
            grad_head,
            preferred_element_type=jnp.float32,
        )
        return (output, logsum, deltas, dquery, ext_dk, ext_dv, glob_dk, glob_dv, rand_dk, rand_dv)

    results = lax.map(
        head_work,
        (
            query_heads,
            grad_heads,
            window[0],
            window[1],
            random_keys,
            random_values,
            global_key_heads,
            global_value_heads,
        ),
    )
    output_heads, logsums, deltas, dquery_heads, ext_dk, ext_dv, glob_dk, glob_dv = results[:8]
    query_total, glob_dk_total, glob_dv_total = lax.psum((query_part, glob_dk, glob_dv), "ctx")
    rim_low = jnp.stack([ext_dk[:, 0], ext_dv[:, 0]], axis=0)
    rim_high = jnp.stack([ext_dk[:, block_count + 1], ext_dv[:, block_count + 1]], axis=0)
    from_next = from_behind(rim_low.astype(jnp.bfloat16), "ctx", -1).astype(rim_low.dtype)
    from_prev = from_behind(rim_high.astype(jnp.bfloat16), "ctx", 1).astype(rim_high.dtype)
    key_heads = ext_dk[:, 1 : block_count + 1]
    value_heads = ext_dv[:, 1 : block_count + 1]
    key_heads = key_heads.at[:, 0].add(from_prev[0]).at[:, block_count - 1].add(from_next[0])
    value_heads = value_heads.at[:, 0].add(from_prev[1]).at[:, block_count - 1].add(from_next[1])
    rand_dk = results[8].reshape(entry_count, BS, DH)
    rand_dv = results[9].reshape(entry_count, BS, DH)
    out_keys = (
        jnp.zeros((ctx_count * capacity, BS, DH), jnp.float32)
        .at[my_place]
        .set(rand_dk)
        .reshape(ctx_count, capacity, BS, DH)
    )
    out_values = (
        jnp.zeros((ctx_count * capacity, BS, DH), jnp.float32)
        .at[my_place]
        .set(rand_dv)
        .reshape(ctx_count, capacity, BS, DH)
    )
    back_keys, back_values = (
        lax.all_to_all(out_keys, "ctx", split_axis=0, concat_axis=0, tiled=True),
        lax.all_to_all(out_values, "ctx", split_axis=0, concat_axis=0, tiled=True),
    )
    back_keys = back_keys.reshape(ctx_count * capacity, BS, DH)
    back_values = back_values.reshape(ctx_count * capacity, BS, DH)
    flat_index = send_index.reshape(-1)
    table_keys = (
        jnp.zeros((block_count * head_count, BS, DH), jnp.float32).at[flat_index].add(back_keys)
    )
    table_values = (
        jnp.zeros((block_count * head_count, BS, DH), jnp.float32).at[flat_index].add(back_values)
    )
    key_heads = key_heads + table_keys.reshape(block_count, head_count, BS, DH).transpose(
        1, 0, 2, 3
    )
    value_heads = value_heads + table_values.reshape(block_count, head_count, BS, DH).transpose(
        1, 0, 2, 3
    )

    def place_global(tensor):
        return jnp.sum(global_hit[None, :, :, None, None] * tensor[:, None], axis=2)

    key_heads = key_heads + place_global(glob_dk_total.reshape(head_count, GLOBAL, BS, DH))
    value_heads = value_heads + place_global(glob_dv_total.reshape(head_count, GLOBAL, BS, DH))
    key_heads = key_heads + key_from_global.reshape(block_count, BS, head_count, DH).transpose(
        2, 0, 1, 3
    )
    value_heads = value_heads + value_from_global.reshape(
        block_count, BS, head_count, DH
    ).transpose(2, 0, 1, 3)
    query_heads_total = dquery_heads + place_global(
        query_total.reshape(GLOBAL, BS, head_count, DH).transpose(2, 0, 1, 3)
    )
    output_total = output_heads.astype(jnp.float32) * keep_rows[None, :, None, None]
    output_total = output_total + place_global(
        global_out.astype(jnp.float32).reshape(GLOBAL, BS, head_count, DH).transpose(2, 0, 1, 3)
    )

    def to_rows(tensor):
        return tensor.transpose(1, 2, 0, 3).reshape(local_rows, features).astype(jnp.bfloat16)

    return (
        to_rows(output_total),
        to_rows(query_heads_total),
        to_rows(key_heads),
        to_rows(value_heads),
    )


Q, K, V, G = range(4)
LOG2E = 1.4426950408889634
VMEM_LIMIT = 40 * 1024 * 1024
GROUP = 4
TILE_W = 256
TILE_D = 128


def peer(step):
    me = lax.axis_index("ctx")
    return (me // 2 + step // 2) % 2 * 2 + (me % 2 + step % 2) % 2


def heads_kernel(
    random_hbm,
    global_hbm,
    q_ref,
    k_ref,
    v_ref,
    g_ref,
    out_ref,
    inb,
    outb,
    scores_buf,
    weights_buf,
    dscores_buf,
    share,
    att_buf,
    dk_acc,
    dv_acc,
    bias,
    k_t,
    v_t,
    own_in,
    own_out,
    in_send,
    in_recv,
    out_send,
    out_recv,
    relay,
    random_ref,
    global_ref,
    list_sem,
):
    n = GROUP
    me = lax.axis_index("ctx")
    rows = q_ref.shape[0]
    seq = n * rows
    blocks = seq // BS
    scaling = DH ** (-0.5)
    sources = (q_ref, k_ref, v_ref, g_ref)

    def at_rows(device):
        return pl.ds(pl.multiple_of(device * rows, rows), rows)

    def at_head(device):
        return pl.ds(pl.multiple_of(device * DH, DH), DH)

    def in_copy(array, step, land):
        other = peer(step)
        return pltpu.make_async_remote_copy(
            src_ref=sources[array].at[:, at_head(other)],
            dst_ref=inb.at[array, at_rows(land)],
            send_sem=in_send.at[array, step - 1],
            recv_sem=in_recv.at[array, step - 1],
            device_id={"ctx": other},
            device_id_type=pl.DeviceIdType.MESH,
        )

    def kind(array):
        return pl.ds(2, 2) if array == 2 else array

    def out_copy(array, step, land):
        other = peer(step)
        return pltpu.make_async_remote_copy(
            src_ref=outb.at[kind(array), at_rows(other)],
            dst_ref=out_ref.at[kind(array), :, at_head(land)],
            send_sem=out_send.at[array, step - 1],
            recv_sem=out_recv.at[array, step - 1],
            device_id={"ctx": other},
            device_id_type=pl.DeviceIdType.MESH,
        )

    def own_copy_in(array):
        return pltpu.make_async_copy(
            sources[array].at[:, at_head(me)], inb.at[array, at_rows(me)], own_in.at[array]
        )

    def own_copy_out(array):
        return pltpu.make_async_copy(
            outb.at[kind(array), at_rows(me)],
            out_ref.at[kind(array), :, at_head(me)],
            own_out.at[array],
        )

    def arrived(array, step):
        if isinstance(step, int) and step == 0:
            own_copy_in(array).wait()
        else:
            in_copy(array, step, peer(step)).wait_recv()

    def leave(array, step):
        own = isinstance(step, int) and step == 0
        (own_copy_out(array) if own else out_copy(array, step, me)).start()

    core = me % 2
    first, last = 3 - core, 2 + core
    barrier = pltpu.get_barrier_semaphore()

    def greet(semaphore, step):
        pl.semaphore_signal(
            semaphore, inc=1, device_id={"ctx": peer(step)}, device_id_type=pl.DeviceIdType.MESH
        )

    def send_rest():
        for array in (K, V):
            in_copy(array, last, me).start()
        for array in (Q, G):
            in_copy(array, first, me).start()
            in_copy(array, last, me).start()

    greet(barrier, 2)

    @pl.when(core == 1)
    def _():
        greet(barrier, 3)
        pl.semaphore_wait(barrier, 1)
        for array in (K, V):
            in_copy(array, 2, me).start()

    @pl.when(core == 0)
    def _():
        pl.semaphore_wait(barrier, 2)
        for array in (K, V):
            in_copy(array, 3, me).start()
        greet(relay, 3)
        send_rest()
        greet(relay, 2)

    random_copy = pltpu.make_async_copy(random_hbm, random_ref, list_sem.at[0])
    global_copy = pltpu.make_async_copy(global_hbm, global_ref, list_sem.at[1])
    random_copy.start()
    global_copy.start()
    for array in (K, V, Q, G):
        own_copy_in(array).start()
    pl.semaphore_wait(relay, 1)

    @pl.when(core == 1)
    def _():
        send_rest()

    for array in (K, V, Q, G):
        in_copy(array, 1, me).start()

    random_copy.wait()
    global_copy.wait()
    key_block = lax.broadcasted_iota(jnp.int32, (blocks, BS), 0)
    global_a, global_b = (global_ref[0], global_ref[1])
    per_device = rows // BS
    for block in range(blocks):
        query_block = jnp.full((blocks, BS), block, jnp.int32)
        named = [(block - 1) % blocks, block, (block + 1) % blocks]
        named += [random_ref[entry, me, block] for entry in range(RAND)]
        named += [global_a, global_b]
        count = sum((key_block == one).astype(jnp.int32) for one in named)
        is_global = (query_block == global_a) | (query_block == global_b)
        count = jnp.where(is_global, 1, count).astype(jnp.float32)
        level = jnp.where(count > 0.5, jnp.log2(jnp.maximum(count, 1.0)), -1e30)
        lanes = slice(block % per_device * BS, block % per_device * BS + BS)
        bias[block // per_device, :, lanes] = level

    contract_last = (((1,), (1,)), ((), ()))

    def folded(tile, combine):
        return combine(tile.reshape(-1, 8, rows), axis=0)

    def weigh(step):
        arrived(Q, step)
        owner = peer(step)
        query = inb[Q, at_rows(owner)]
        highest = jnp.full((8, rows), -3e38, jnp.float32)
        for start in range(0, seq, TILE_W):
            part = slice(start, start + TILE_W)
            scores = lax.dot_general(
                inb[K, part], query, contract_last, preferred_element_type=jnp.float32
            )
            level = bias[owner, start // BS : (start + TILE_W) // BS]
            scores = (
                scores.reshape(-1, BS, rows) * (scaling * LOG2E) + level[:, None, :]
            ).reshape(TILE_W, rows)
            scores_buf[part] = scores
            highest = jnp.maximum(highest, folded(scores, jnp.max))
        highest = jnp.max(highest, axis=0, keepdims=True)
        total = jnp.zeros((8, rows), jnp.float32)
        for start in range(0, seq, TILE_W):
            part = slice(start, start + TILE_W)
            weights = jnp.exp2(scores_buf[part] - highest)
            total = total + folded(weights, jnp.sum)
            weights_buf[step, part] = weights.astype(jnp.bfloat16)
        share[step] = 1.0 / jnp.sum(total, axis=0, keepdims=True)

    def attend(step):
        att_t = jnp.dot(v_t[...], weights_buf[step], preferred_element_type=jnp.float32)
        att_t = (att_t * share[step]).astype(jnp.bfloat16).astype(jnp.float32)
        outb[0, at_rows(peer(step))] = att_t.T.astype(jnp.bfloat16)
        att_buf[step] = att_t
        leave(0, step)

    def differentiate(step, opening):
        arrived(G, step)
        owner = peer(step)
        query_t = inb[Q, at_rows(owner)].astype(jnp.float32).T
        grad = inb[G, at_rows(owner)]
        grad_t = grad.astype(jnp.float32).T
        delta = jnp.sum(grad_t * att_buf[step], axis=0, keepdims=True)
        for start in range(0, seq, TILE_D):
            part = slice(start, start + TILE_D)
            dprobs = lax.dot_general(
                inb[V, part], grad, contract_last, preferred_element_type=jnp.float32
            )
            weights = weights_buf[step, part].astype(jnp.float32)
            dscores_buf[part] = (weights * (dprobs - delta)).astype(jnp.bfloat16)
        dq_t = jnp.dot(k_t[...], dscores_buf[...], preferred_element_type=jnp.float32)
        dq_t = dq_t * (share[step] * scaling)
        outb[1, at_rows(owner)] = dq_t.T.astype(jnp.bfloat16)
        leave(1, step)
        grad_share = (grad_t * share[step]).astype(jnp.bfloat16)
        query_share = (query_t * share[step]).astype(jnp.bfloat16)
        dv = lax.dot_general(
            weights_buf[step], grad_share, contract_last, preferred_element_type=jnp.float32
        )
        dk = lax.dot_general(
            dscores_buf[...], query_share, contract_last, preferred_element_type=jnp.float32
        )
        dv_acc[...] = dv if opening else dv_acc[...] + dv
        dk_acc[...] = dk if opening else dk_acc[...] + dk

    for step in range(n):
        arrived(K, step)
    k_t[...] = inb[K].T
    weigh(0)
    weigh(1)
    for step in range(n):
        arrived(V, step)
    v_t[...] = inb[V].T
    attend(0)
    differentiate(0, True)
    for step in (first, last):
        weigh(step)
        attend(step)
    differentiate(first, False)
    attend(1)
    differentiate(1, False)
    differentiate(last, False)

    outb[2] = (dk_acc[...] * scaling).astype(jnp.bfloat16)
    outb[3] = dv_acc[...].astype(jnp.bfloat16)
    for step in (2, 3, 1, 0):
        leave(2, step)

    for array in range(4):
        for step in range(1, n):
            in_copy(array, step, me).wait_send()
    for array in range(3):
        own_copy_out(array).wait()
        for step in range(1, n):
            out_copy(array, step, me).wait_send()
            out_copy(array, step, peer(step)).wait_recv()


def place_kernel(joint_ref, *refs):
    copies = [
        pltpu.make_async_copy(joint_ref.at[array], refs[array], refs[4].at[array])
        for array in range(4)
    ]
    for copy in copies:
        copy.start()
    for copy in copies:
        copy.wait()


def by_heads(queries, keys, values, out_grad, random_blocks, global_blocks):
    n = GROUP
    rows, features = queries.shape
    seq = n * rows
    blocks = seq // BS
    anywhere = pl.BlockSpec(memory_space=pl.ANY)
    result = pl.pallas_call(
        heads_kernel,
        out_shape=jax.ShapeDtypeStruct((4, rows, features), jnp.bfloat16),
        in_specs=[anywhere] * 6,
        out_specs=anywhere,
        scratch_shapes=[
            pltpu.VMEM((4, seq, DH), jnp.bfloat16),
            pltpu.VMEM((4, seq, DH), jnp.bfloat16),
            pltpu.VMEM((seq, rows), jnp.float32),
            pltpu.VMEM((n, seq, rows), jnp.bfloat16),
            pltpu.VMEM((seq, rows), jnp.bfloat16),
            pltpu.VMEM((n, 1, rows), jnp.float32),
            pltpu.VMEM((n, DH, rows), jnp.float32),
            pltpu.VMEM((seq, DH), jnp.float32),
            pltpu.VMEM((seq, DH), jnp.float32),
            pltpu.VMEM((n, blocks, rows), jnp.float32),
            pltpu.VMEM((DH, seq), jnp.bfloat16),
            pltpu.VMEM((DH, seq), jnp.bfloat16),
            pltpu.SemaphoreType.DMA((4,)),
            pltpu.SemaphoreType.DMA((4,)),
            pltpu.SemaphoreType.DMA((4, n - 1)),
            pltpu.SemaphoreType.DMA((4, n - 1)),
            pltpu.SemaphoreType.DMA((4, n - 1)),
            pltpu.SemaphoreType.DMA((4, n - 1)),
            pltpu.SemaphoreType.REGULAR,
            pltpu.SMEM((RAND, n, blocks), jnp.int32),
            pltpu.SMEM((GLOBAL,), jnp.int32),
            pltpu.SemaphoreType.DMA((2,)),
        ],
        compiler_params=pltpu.CompilerParams(
            collective_id=0, has_side_effects=True, vmem_limit_bytes=VMEM_LIMIT
        ),
    )(
        *(
            pltpu.with_memory_space_constraint(array, pltpu.HBM)
            for array in (
                random_blocks.transpose(2, 0, 1),
                global_blocks,
                queries,
                keys,
                values,
                out_grad,
            )
        )
    )
    return pl.pallas_call(
        place_kernel,
        out_shape=[jax.ShapeDtypeStruct((rows, features), jnp.bfloat16)] * 4,
        in_specs=[anywhere],
        out_specs=[anywhere] * 4,
        scratch_shapes=[pltpu.SemaphoreType.DMA((4,))],
        compiler_params=pltpu.CompilerParams(vmem_limit_bytes=VMEM_LIMIT),
    )(result)


def solution(mesh):
    in_specs = (
        P(("dp", "ctx"), "head"),
        P(("dp", "ctx"), "head"),
        P(("dp", "ctx"), "head"),
        P(("dp", "ctx"), "head"),
        P(("dp", "head"), None, None),
        P("dp"),
    )
    out_specs = (
        P(("dp", "ctx"), "head"),
        P(("dp", "ctx"), "head"),
        P(("dp", "ctx"), "head"),
        P(("dp", "ctx"), "head"),
    )
    ctx_count = mesh.shape["ctx"]

    def body(queries, *rest):
        heads = queries.shape[1] // DH
        if heads == ctx_count == GROUP:
            return by_heads(queries, *rest)
        return on_device(queries, *rest)

    return jax.shard_map(
        body, mesh=mesh, in_specs=in_specs, out_specs=out_specs, check_vma=False
    )
```
